32 devices in a mesh: dp: 4 (over x, core), fsdp: 8 (over z, y).
Axes of the slice: x: 2, y: 2, z: 4, core: 2. Of those that a mesh axis runs over, the one named last changes fastest.
Arguments:
- token_ids: int32 [4096], P('dp'), may hold values from 0 to 15263, as said below
- embed_table: bfloat16 [15264, 768], P('fsdp'), may hold values from -16 to 16, as said below
- w_qkv: bfloat16 [768, 2304], P('fsdp'), may hold values from -2 to 2
- w_out: bfloat16 [768, 768], P('fsdp'), may hold values from -0.21875 to 0.21875
- ln_gain: float32 [768], replicated, may hold values from 0.5 to 1.5
- ln_bias: float32 [768], replicated, may hold values from -1 to 1
- centroids_t: bfloat16 [768, 32768], P('fsdp', 'dp'), may hold values from -24 to 24
- assignments: int32 [4096], replicated, may hold values from 0 to 32767, as said below
Outputs:
- token_loss: float32 [4096], P(('dp', 'fsdp'))
- new_centroids: float32 [32768, 768], P(('dp', 'fsdp'))
The draws below stay inside these ranges and needn't reach their ends.
Inputs may be any that keep to these rules, and one draw needn't show every extreme that they name: `token_ids`: id 0 is padding; a passage may end in a run of padding. `embed_table`: token embeddings of order one. `assignments`: cluster sizes are skewed.
All inputs are finite; a program needn't handle non-finite values.
Results may differ from the reference program's by a relative error of at most 0.0055.
Values may be sent and summed in bfloat16 or wider, within the bound.
A program may use at most 64 MiB of HBM per device.

```python
import math
import jax
import jax.numpy as jnp
from jax import lax

D = 768
HEADS = 12
HEAD = 64
VOCAB = 15264
SEQ = 128
CENT = 32768
TOKENS = 4096


def shared_bias(key):
    spread = 0.1
    return spread * jax.random.normal(jax.random.fold_in(key, 7), (D,), jnp.float32)


def skewed_ranks(key, count, limit):
    levels = (limit - 1).bit_length()
    level = jax.random.randint(jax.random.fold_in(key, 1), (count,), 0, levels + 1).astype(jnp.int32)
    upper = jnp.minimum(jnp.left_shift(jnp.ones((count,), jnp.int32), level), limit).astype(jnp.int32)
    return jax.random.randint(jax.random.fold_in(key, 2), (count,), 0, upper).astype(jnp.int32)


def draw_token_ids(key, part):
    passages = TOKENS // SEQ
    ranks = skewed_ranks(jax.random.fold_in(key, 31), TOKENS, VOCAB - 1)
    order = jax.random.permutation(jax.random.fold_in(key, 32), VOCAB - 1).astype(jnp.int32)
    words = order[ranks] + 1
    lengths = jax.random.randint(jax.random.fold_in(key, 33), (passages, 1), SEQ // 8, SEQ + 1).astype(jnp.int32)
    positions = jnp.arange(SEQ, dtype=jnp.int32)
    padded = positions[None, :] >= lengths
    words = jnp.where(padded, jnp.zeros_like(words.reshape(passages, SEQ)), words.reshape(passages, SEQ))
    return words.reshape(TOKENS).astype(jnp.int32)


def draw_assignments(key, part):
    ranks = skewed_ranks(jax.random.fold_in(key, 41), TOKENS, CENT)
    order = jax.random.permutation(jax.random.fold_in(key, 42), CENT).astype(jnp.int32)
    spread_part = order[ranks]
    span = CENT // 8
    first = jax.random.randint(jax.random.fold_in(key, 43), (), 0, 8).astype(jnp.int32) * span
    crowded = first + jax.random.randint(jax.random.fold_in(key, 44), (TOKENS,), 0, span).astype(jnp.int32)
    chosen = jax.random.permutation(jax.random.fold_in(key, 45), TOKENS).astype(jnp.int32) < TOKENS // 4
    return jnp.where(chosen, crowded, spread_part).astype(jnp.int32)


def draw_ln_bias(key, part):
    return shared_bias(key).astype(jnp.float32)


def draw_embed_table(key, part):
    values = jax.random.normal(jax.random.fold_in(key, 3), (VOCAB, D), jnp.float32)
    values = jnp.clip(values, -5.0, 5.0)
    return values.astype(jnp.bfloat16)


def draw_w_qkv(key, part):
    factor = 1.0 / jnp.sqrt(jnp.float32(D))
    parts = jnp.clip(jax.random.normal(jax.random.fold_in(key, 5), (D, 3 * D), jnp.float32), -5.0, 5.0) * factor
    return parts.astype(jnp.bfloat16)


def draw_centroids_t(key, part):
    values = 0.1 * jnp.clip(jax.random.normal(jax.random.fold_in(key, 11), (D, CENT), jnp.float32), -5.0, 5.0)
    return values.astype(jnp.bfloat16)


def block_levels(stream_key, dims, cuts, smallest, top_value):
    def one(axis_at, shards_of):
        heights = jax.random.uniform(jax.random.fold_in(jax.random.fold_in(stream_key, 6), axis_at), (shards_of,), jnp.float32, smallest / len(cuts), top_value / len(cuts))
        return jnp.repeat(jnp.exp(heights), dims[axis_at] // shards_of).reshape((-1,) + (1,) * (len(dims) - axis_at - 1))

    factor_of = one(*cuts[0])
    for cut in cuts[1:]:
        factor_of = factor_of * one(*cut)
    return factor_of


def centred(key, extent, deviation, most, cuts=(), kind=jnp.bfloat16):
    values = jax.random.normal(key, extent, jnp.float32) * deviation
    if len(cuts) > 0:
        values = block_levels(key, extent, cuts, -0.22, 0.18) * values
    return jnp.clip(values, min=-most, max=most).astype(kind)


def setup_inputs(seed: int = 0) -> dict:
    key_of = jax.random.split(jax.random.key(seed), 9)
    token_ids = draw_token_ids(jax.random.fold_in(key_of[8], 71), 0)
    embed_table = draw_embed_table(jax.random.fold_in(key_of[8], 71), 0)
    w_qkv = draw_w_qkv(jax.random.fold_in(key_of[8], 71), 0)
    w_out = centred(key_of[3], (D, D), D ** -0.5, 0.21875, ((0, 8),))
    ln_gain = jnp.clip(1.0 + 0.1 * jax.random.normal(key_of[4], (D,), jnp.float32), 0.5, 1.5)
    ln_bias = draw_ln_bias(jax.random.fold_in(key_of[8], 71), 0)
    centroids_t = draw_centroids_t(jax.random.fold_in(key_of[8], 71), 0)
    assignments = draw_assignments(jax.random.fold_in(key_of[8], 71), 0)
    return dict(token_ids=token_ids, embed_table=embed_table, w_qkv=w_qkv, w_out=w_out, ln_gain=ln_gain, ln_bias=ln_bias, centroids_t=centroids_t, assignments=assignments)


def layer_norm(values, ln_gain, ln_bias):
    center = values - lax.optimization_barrier(jnp.mean(values, axis=-1, keepdims=True))
    spread = lax.optimization_barrier(jnp.mean(center * center, axis=-1, keepdims=True))
    return center * lax.rsqrt(spread + 1e-05) * ln_gain + ln_bias

def reference(token_ids, embed_table, w_qkv, w_out, ln_gain, ln_bias, centroids_t, assignments):
    inputs = embed_table[token_ids]
    passages = TOKENS // SEQ
    packed = jnp.dot(inputs, w_qkv, preferred_element_type=jnp.float32).astype(jnp.bfloat16)
    packed = packed.reshape(passages, SEQ, 3, HEADS, HEAD).astype(jnp.float32)
    scores = jnp.einsum('bqhd,bkhd->bhqk', packed[:, :, 0], packed[:, :, 1]) * (1.0 / math.sqrt(HEAD))
    probs = jax.nn.softmax(scores, axis=-1).astype(jnp.bfloat16)
    context = jnp.einsum('bhqk,bkhd->bqhd', probs.astype(jnp.float32), packed[:, :, 2])
    context = context.astype(jnp.bfloat16).reshape(TOKENS, D)
    mixed = jnp.dot(context, w_out, preferred_element_type=jnp.float32) + inputs.astype(jnp.float32)
    embedded = layer_norm(mixed, ln_gain, ln_bias).astype(jnp.bfloat16)
    block = math.gcd(TOKENS, 512)

    def score_rows(pieces):
        rows, assigned = pieces
        logits = jnp.dot(rows, centroids_t, preferred_element_type=jnp.float32)
        peak = lax.optimization_barrier(jnp.max(logits, axis=1))
        total = jnp.log(lax.optimization_barrier(jnp.sum(jnp.exp(logits - peak[:, None]), axis=1))) + peak
        chosen = jnp.take_along_axis(logits, assigned[:, None], axis=1)[:, 0]
        return total - chosen
    token_loss = lax.map(score_rows, (embedded.reshape(TOKENS // block, block, D), assignments.reshape(TOKENS // block, block))).reshape(TOKENS)
    sums = jax.ops.segment_sum(embedded.astype(jnp.float32), assignments, num_segments=CENT)
    counts = jax.ops.segment_sum(jnp.ones((TOKENS,), jnp.int32), assignments, num_segments=CENT)
    previous = centroids_t.T.astype(jnp.float32)
    new_centroids = jnp.where(counts[:, None] > 0, sums / jnp.maximum(counts, 1)[:, None].astype(jnp.float32), previous)
    return (token_loss, new_centroids)
```

```python
import functools
import math

import jax
import jax.numpy as jnp
from jax import lax
from jax.experimental import pallas as pl
from jax.experimental.pallas import tpu as pltpu
from jax.sharding import PartitionSpec as P

HEADS = 12
HEAD = 64
SEQ = 128


def joined(shard, axis, combine):
    everything = jax.tree.map(lambda part: lax.all_gather(part, axis), shard)
    initial = jax.tree.map(lambda part: part[0], everything)

    def lap(k, so_far):
        return combine(so_far, jax.tree.map(lambda part: part[k], everything))

    return lax.fori_loop(1, lax.axis_size(axis), lap, initial)


def layer_norm(values, ln_gain, ln_bias):
    center = values - jnp.mean(values, axis=-1, keepdims=True)
    spread = jnp.mean(center * center, axis=-1, keepdims=True)
    return center * lax.rsqrt(spread + 1e-05) * ln_gain + ln_bias


def encode(inputs, qkv_full, out_full, ln_gain, ln_bias):
    passages = inputs.shape[0] // SEQ
    packed = jnp.dot(inputs, qkv_full, preferred_element_type=jnp.float32).astype(jnp.bfloat16)
    packed = packed.reshape(passages, SEQ, 3, HEADS, HEAD)
    scores = jnp.einsum(
        "bqhd,bkhd->bhqk", packed[:, :, 0], packed[:, :, 1], preferred_element_type=jnp.float32
    ) * (1.0 / math.sqrt(HEAD))
    probs = jax.nn.softmax(scores, axis=-1).astype(jnp.bfloat16)
    context = jnp.einsum(
        "bhqk,bkhd->bqhd", probs, packed[:, :, 2], preferred_element_type=jnp.float32
    )
    context = context.astype(jnp.bfloat16).reshape(inputs.shape[0], HEADS * HEAD)
    mixed = jnp.dot(context, out_full, preferred_element_type=jnp.float32) + inputs.astype(
        jnp.float32
    )
    return layer_norm(mixed, ln_gain, ln_bias).astype(jnp.bfloat16)


def one_hot_sums(rows, targets, width):
    count = rows.shape[0]
    step_rows = math.gcd(count, 512)
    columns = jnp.arange(width, dtype=jnp.int32)

    def one_visit(totals, pieces):
        block_rows, block_targets = pieces
        hits = (block_targets[:, None] == columns[None, :]).astype(jnp.bfloat16)
        return (
            totals
            + lax.dot_general(
                hits, block_rows, (((0,), (0,)), ((), ())), preferred_element_type=jnp.float32
            ),
            None,
        )

    start = jnp.zeros((width, rows.shape[1]), jnp.float32)
    totals, unused = lax.scan(
        one_visit,
        start,
        (
            rows.reshape(count // step_rows, step_rows, rows.shape[1]),
            targets.reshape(count // step_rows, step_rows),
        ),
    )
    return totals


def combine_parts(first, second):
    peak = jnp.maximum(first[0], second[0])
    mass = first[1] * jnp.exp(first[0] - peak) + second[1] * jnp.exp(second[0] - peak)
    return (peak, mass, first[2] + second[2])


def shards(token_ids, embed_table, w_qkv, w_out, ln_gain, ln_bias, centroids_t, assignments):
    dp_size = lax.axis_size("dp")
    fsdp_size = lax.axis_size("fsdp")
    dp_rank = lax.axis_index("dp")
    fsdp_rank = lax.axis_index("fsdp")
    vocab_rows = embed_table.shape[0]
    local_ids = token_ids - fsdp_rank * vocab_rows
    inside = (local_ids >= 0) & (local_ids < vocab_rows)
    looked = jnp.take(embed_table, jnp.clip(local_ids, 0, vocab_rows - 1), axis=0)
    looked = jnp.where(inside[:, None], looked, jnp.zeros_like(looked))
    inputs = (
        lax.psum_scatter(looked, "fsdp", scatter_dimension=0, tiled=True)
        .astype(jnp.float32)
        .astype(jnp.bfloat16)
    )
    qkv_full, out_full, cent_full = (
        lax.all_gather(w_qkv, "fsdp", axis=0, tiled=True),
        lax.all_gather(w_out, "fsdp", axis=0, tiled=True),
        lax.all_gather(centroids_t, "fsdp", axis=0, tiled=True),
    )
    encoded = encode(inputs, qkv_full, out_full, ln_gain, ln_bias)
    own_rows = encoded.shape[0]
    width = encoded.shape[1]
    block_width = cent_full.shape[1]
    per_dev = block_width // fsdp_size
    slab = lax.all_gather(encoded, "dp", axis=0, tiled=True)
    slab_assign = lax.dynamic_index_in_dim(
        assignments.reshape(dp_size, fsdp_size, own_rows), fsdp_rank, 1, keepdims=False
    ).reshape(-1)
    owned = slab_assign - dp_rank * block_width
    slab_rows = slab.shape[0]
    step_rows = math.gcd(slab_rows, 512)
    columns = jnp.arange(block_width, dtype=jnp.int32)

    def body_visit(totals, pieces):
        block_rows, local = pieces
        logits = jnp.dot(block_rows, cent_full, preferred_element_type=jnp.float32)
        peak = jnp.max(logits, axis=1)
        mass = jnp.sum(jnp.exp(logits - peak[:, None]), axis=1)
        hits = local[:, None] == columns[None, :]
        picked = jnp.sum(jnp.where(hits, logits, 0.0), axis=1)
        return (totals, (peak, mass, picked))

    start = jnp.zeros((1,), jnp.float32)
    partial_value, stats = lax.scan(
        body_visit,
        start,
        (
            slab.reshape(slab_rows // step_rows, step_rows, width),
            owned.reshape(slab_rows // step_rows, step_rows),
        ),
    )
    peaks, masses, picks = (stats[0].reshape(-1), stats[1].reshape(-1), stats[2].reshape(-1))
    peaks, masses, picks = joined((peaks, masses, picks), "dp", combine_parts)
    peak_own = lax.dynamic_slice_in_dim(peaks, dp_rank * own_rows, own_rows)
    mass_own = lax.dynamic_slice_in_dim(masses, dp_rank * own_rows, own_rows)
    pick_own = lax.dynamic_slice_in_dim(picks, dp_rank * own_rows, own_rows)
    token_loss = jnp.log(mass_own) + peak_own - pick_own
    share = lax.all_to_all(encoded, "fsdp", split_axis=1, concat_axis=0, tiled=True)
    every_rows = lax.all_gather(share, "dp", axis=0, tiled=True)
    block_local = assignments - dp_rank * block_width
    partial_share = one_hot_sums(every_rows, block_local, block_width)
    totals = lax.all_to_all(partial_share, "fsdp", split_axis=0, concat_axis=1, tiled=True)
    base = dp_rank * block_width + fsdp_rank * per_dev
    targets = base + jnp.arange(per_dev, dtype=jnp.int32)
    counts = jnp.sum((assignments[:, None] == targets[None, :]).astype(jnp.int32), axis=0)
    previous = lax.dynamic_slice_in_dim(cent_full, fsdp_rank * per_dev, per_dev, 1).T.astype(
        jnp.float32
    )
    new_centroids = jnp.where(
        counts[:, None] > 0, totals / jnp.maximum(counts, 1)[:, None].astype(jnp.float32), previous
    )
    return (token_loss, new_centroids)


VMEM_LIMIT = 60 * 1024 * 1024
WHOLE_VMEM = pl.BlockSpec(memory_space=pltpu.VMEM)


class Place:
    def __init__(self, deep):
        self.deep = deep
        self.dp, self.fsdp = lax.axis_index("dp"), lax.axis_index("fsdp")
        self.x, self.c = self.dp // 2, self.dp % 2
        self.z, self.y = self.fsdp // 2, self.fsdp % 2

    def at(self, x=None, c=None, z=None, y=None):
        x, c = self.x if x is None else x, self.c if c is None else c
        z, y = self.z if z is None else z, self.y if y is None else y
        return {"dp": x * 2 + c, "fsdp": z * 2 + y}

    def greet(self):
        barrier = pltpu.get_barrier_semaphore()
        peers = [self.at(x=1 - self.x), self.at(c=1 - self.c), self.at(y=1 - self.y)]
        peers += [self.at(z=(self.z + k) % self.deep) for k in range(1, self.deep)]
        for peer in peers:
            pl.semaphore_signal(barrier, inc=1, device_id=peer, device_id_type=pl.DeviceIdType.MESH)
        pl.semaphore_wait(barrier, len(peers))


class Sender:
    def __init__(self, sems):
        self.sems, self.used, self.sent = sems, 0, []

    def send(self, src, dst, recv_sem, peer, when=None):
        copy = pltpu.make_async_remote_copy(
            src_ref=src,
            dst_ref=dst,
            send_sem=self.sems.at[self.used],
            recv_sem=recv_sem,
            device_id=peer,
            device_id_type=pl.DeviceIdType.MESH,
        )
        self.used += 1
        self.sent.append((copy, when))
        guarded(when, copy.start)

    def arrived(self, dst, recv_sem, peer, when=None):
        copy = pltpu.make_async_remote_copy(
            src_ref=dst,
            dst_ref=dst,
            send_sem=self.sems.at[0],
            recv_sem=recv_sem,
            device_id=peer,
            device_id_type=pl.DeviceIdType.MESH,
        )
        guarded(when, copy.wait_recv)

    def drain(self):
        for copy, when in self.sent:
            guarded(when, copy.wait_send)


def guarded(when, action):
    if when is None:
        action()
    else:
        pl.when(when)(action)


def prepare_kernel(
    deep, rows_ref, mine_ref, inputs_ref, w_ref, from_y, joined_y, from_z, send_sems, y_sems, z_sems, w_sems
):
    place = Place(deep)
    place.greet()
    out = Sender(send_sems)
    x, c, z, y = place.x, place.c, place.z, place.y
    quarter, across = x * 2 + c, (1 - x) * 2 + c
    own = place.fsdp
    for k in range(1, deep + 1):
        to = (z + k) % deep
        out.send(rows_ref.at[to * 2 + (1 - y)], from_y.at[to], y_sems.at[to], place.at(y=1 - y))
    up, down = place.at(z=jnp.minimum(z + 1, deep - 1)), place.at(z=jnp.maximum(z - 1, 0))

    def share(q, s, src, to_y):
        if to_y:
            out.send(src, w_ref.at[q, s], w_sems.at[q, s], place.at(y=1 - y))

    mine = mine_ref.at[quarter]
    out.send(mine, w_ref.at[quarter, own], w_sems.at[quarter, own], up, z + 1 < deep)
    out.send(mine, w_ref.at[quarter, own], w_sems.at[quarter, own], down, z > 0)

    def spread(s, when=None):
        block = w_ref.at[quarter, s]
        out.send(block, block, w_sems.at[quarter, s], place.at(x=1 - x), when)
        out.send(block, block, w_sems.at[quarter, s], place.at(c=1 - c), when)

    for k in range(1, deep):
        for sign in (-1, 1):
            have = (z + sign * k >= 0) & (z + sign * k < deep)
            z0 = jnp.clip(z + sign * k, 0, deep - 1)
            s = z0 * 2 + y
            block = w_ref.at[quarter, s]
            out.arrived(block, w_sems.at[quarter, s], place.at(y=1 - y), have)
            onward = have & (z + 1 < deep) if sign < 0 else have & (z > 0)
            if k < deep - 1:
                out.send(block, block, w_sems.at[quarter, s], up if sign < 0 else down, onward)
            spread(s, have)
    for q in range(4):
        w_ref[q, own] = mine_ref[q]
    for k in range(1, deep + 1):
        to = (z + k) % deep
        out.arrived(from_y.at[to], y_sems.at[to], place.at(y=1 - y))
        if k < deep:
            joined_y[to] = from_y[to] + rows_ref[to * 2 + y]
            out.send(joined_y.at[to], from_z.at[deep - k], z_sems.at[deep - k], place.at(z=to))
    out.send(mine, w_ref.at[quarter, own], w_sems.at[quarter, own], place.at(y=1 - y))
    for k in range(1, deep):
        s = (z + k) % deep * 2 + y
        block = w_ref.at[quarter, s]
        out.send(block, block, w_sems.at[quarter, s], place.at(y=1 - y))
    for k in range(deep):
        s = (z + k) % deep * 2 + (1 - y)
        out.arrived(w_ref.at[quarter, s], w_sems.at[quarter, s], place.at(y=1 - y))
        spread(s)
    others = [(z + k) % deep * 2 + y for k in range(1, deep)]
    others += [(z + k) % deep * 2 + (1 - y) for k in range(deep)]
    for s in others:
        block = w_ref.at[across, s]
        out.arrived(block, w_sems.at[across, s], place.at(x=1 - x))
        out.send(block, block, w_sems.at[across, s], place.at(c=1 - c))
    total = from_y[z] + rows_ref[own]
    for k in range(1, deep):
        out.arrived(from_z.at[k], z_sems.at[k], place.at(y=1 - y))
        total = total + from_z[k]
    inputs_ref[...] = total
    for q in (x * 2 + (1 - c), (1 - x) * 2 + (1 - c)):
        for s in others:
            out.arrived(w_ref.at[q, s], w_sems.at[q, s], place.at(c=1 - c))
    out.drain()


def prepare(rows, mine, deep):
    parts, own_rows, width = rows.shape
    feats = mine.shape[1]
    return pl.pallas_call(
        functools.partial(prepare_kernel, deep),
        out_shape=(
            jax.ShapeDtypeStruct((own_rows, width), rows.dtype),
            jax.ShapeDtypeStruct((4, parts, feats, width), mine.dtype),
        ),
        in_specs=[WHOLE_VMEM] * 2,
        out_specs=(WHOLE_VMEM, WHOLE_VMEM),
        scratch_shapes=[
            pltpu.VMEM((deep, own_rows, width), rows.dtype),
            pltpu.VMEM((deep, own_rows, width), rows.dtype),
            pltpu.VMEM((deep, own_rows, width), rows.dtype),
            pltpu.SemaphoreType.DMA((16 * deep,)),
            pltpu.SemaphoreType.DMA((deep,)),
            pltpu.SemaphoreType.DMA((deep,)),
            pltpu.SemaphoreType.DMA((4, parts)),
        ],
        compiler_params=pltpu.CompilerParams(
            collective_id=0, has_side_effects=True, vmem_limit_bytes=VMEM_LIMIT
        ),
        name="prepare",
    )(rows, mine)


def tokens_kernel(deep, mine_ref, all_ref, send_sems, recv_sems):
    place = Place(deep)
    place.greet()
    out = Sender(send_sems)
    x, c, z, y = place.x, place.c, place.z, place.y
    x_first = c == 1
    second_xy = (jnp.where(x_first, 1 - x, x), jnp.where(x_first, y, 1 - y))
    third_xy = (jnp.where(x_first, x, 1 - x), jnp.where(x_first, 1 - y, y))
    second = place.at(x=second_xy[0], y=second_xy[1])
    third = place.at(x=third_xy[0], y=third_xy[1])
    partner = place.at(c=1 - c)
    up, down = place.at(z=jnp.minimum(z + 1, deep - 1)), place.at(z=jnp.maximum(z - 1, 0))

    def number(x0, c0, z0, y0):
        return ((x0 * 2 + c0) * deep + z0) * 2 + y0

    def push(b, peer, when=None, src=None):
        block = all_ref.at[b]
        out.send(block if src is None else src, block, recv_sems.at[b], peer, when)

    def wait(b, when=None):
        out.arrived(all_ref.at[b], recv_sems.at[b], partner, when)

    own = number(x, c, z, y)
    push(own, up, z + 1 < deep, mine_ref)
    push(own, down, z > 0, mine_ref)
    for peer in (second, third, partner):
        push(own, peer, None, mine_ref)
    all_ref[own] = mine_ref[...]
    order = [(z, None, 0)]
    for k in range(1, deep):
        for sign in (-1, 1):
            have = (z + sign * k >= 0) & (z + sign * k < deep)
            order.append((jnp.clip(z + sign * k, 0, deep - 1), have, sign))
    for at, (z0, have, sign) in enumerate(order):
        if at > 0:
            b = number(x, c, z0, y)
            wait(b, have)
            if at + 2 < len(order):
                push(b, up if sign < 0 else down, have & ((z + 1 < deep) if sign < 0 else (z > 0)))
            push(b, second, have)
            push(b, third, have)
            push(b, partner, have)
        b = number(second_xy[0], c, z0, second_xy[1])
        wait(b, have)
        push(b, third, have)
        push(b, partner, have)
        lag = [order[at - 2]] if at >= 2 else []
        lag += order[-2:] if at == len(order) - 1 else []
        for z1, have1, unused in lag:
            for second_way in (False, True):
                xx, yy = third_xy
                if second_way:
                    xx, yy = 1 - x, 1 - y
                b = number(xx, c, z1, yy)
                wait(b, have1)
                push(b, partner, have1)
    for k in range(deep):
        for x0 in range(2):
            for y0 in range(2):
                wait(number(x0, 1 - c, k, y0))
    out.drain()


def every_token(mine, deep):
    rows, width = mine.shape
    blocks = 8 * deep
    return pl.pallas_call(
        functools.partial(tokens_kernel, deep),
        out_shape=jax.ShapeDtypeStruct((blocks, rows, width), mine.dtype),
        in_specs=[WHOLE_VMEM],
        out_specs=WHOLE_VMEM,
        scratch_shapes=[
            pltpu.SemaphoreType.DMA((24 * deep,)),
            pltpu.SemaphoreType.DMA((blocks,)),
        ],
        compiler_params=pltpu.CompilerParams(
            collective_id=1, has_side_effects=True, vmem_limit_bytes=VMEM_LIMIT
        ),
        name="every_token",
    )(mine)


def owner_kernel(steps, assign_ref, tokens_ref, cent_ref, peak_ref, mass_ref, pick_ref, new_ref, old, counts):
    step = pl.program_id(0)

    @pl.when(step == 0)
    def first():
        old[...] = cent_ref[...].T
        new_ref[...] = jnp.zeros_like(new_ref)
        counts[...] = jnp.zeros_like(counts)

    rows = tokens_ref[...]
    logits = lax.dot_general(
        old[...], rows, (((1,), (1,)), ((), ())), preferred_element_type=jnp.float32
    )
    peak = jnp.max(logits, axis=0, keepdims=True)
    peak_ref[0] = peak
    mass_ref[0] = jnp.sum(jnp.exp(logits - peak), axis=0, keepdims=True)
    hits = lax.broadcasted_iota(jnp.int32, logits.shape, 0) == assign_ref[0]
    pick_ref[0] = jnp.sum(jnp.where(hits, logits, 0.0), axis=0, keepdims=True)
    ones = jnp.where(hits, 1.0, 0.0)
    counts[...] += jnp.sum(ones, axis=1, keepdims=True)
    new_ref[...] += jnp.dot(ones.astype(jnp.bfloat16), rows, preferred_element_type=jnp.float32)

    @pl.when(step == steps - 1)
    def last():
        many = counts[...]
        new_ref[...] = jnp.where(
            many > 0, new_ref[...] / jnp.maximum(many, 1.0), old[...].astype(jnp.float32)
        )


def owner(tokens, cent, local_assign):
    count, width = tokens.shape
    per_dev = cent.shape[1]
    block = math.gcd(count, 512)
    steps = count // block
    row = pl.BlockSpec((1, 1, block), lambda i: (i, 0, 0))
    stat = jax.ShapeDtypeStruct((steps, 1, block), jnp.float32)
    peak, mass, pick, new = pl.pallas_call(
        functools.partial(owner_kernel, steps),
        out_shape=(stat, stat, stat, jax.ShapeDtypeStruct((per_dev, width), jnp.float32)),
        grid=(steps,),
        in_specs=[
            row,
            pl.BlockSpec((block, width), lambda i: (i, 0)),
            pl.BlockSpec((width, per_dev), lambda i: (0, 0)),
        ],
        out_specs=(row, row, row, pl.BlockSpec((per_dev, width), lambda i: (0, 0))),
        scratch_shapes=[
            pltpu.VMEM((per_dev, width), cent.dtype),
            pltpu.VMEM((per_dev, 1), jnp.float32),
        ],
        compiler_params=pltpu.CompilerParams(vmem_limit_bytes=VMEM_LIMIT),
        name="owner",
    )(local_assign.reshape(steps, 1, block), tokens, cent)
    return peak.reshape(-1), mass.reshape(-1), pick.reshape(-1), new


def token_shards(token_ids, embed_table, w_qkv, w_out, ln_gain, ln_bias, centroids_t, assignments):
    dp_size, fsdp_size = lax.axis_size("dp"), lax.axis_size("fsdp")
    dp_rank, fsdp_rank = lax.axis_index("dp"), lax.axis_index("fsdp")
    deep = fsdp_size // 2
    vocab_rows, width = embed_table.shape
    own_rows = token_ids.shape[0] // fsdp_size
    local_ids = token_ids - fsdp_rank * vocab_rows
    inside = (local_ids >= 0) & (local_ids < vocab_rows)
    looked = jnp.take(embed_table, jnp.clip(local_ids, 0, vocab_rows - 1), axis=0)
    looked = jnp.where(inside[:, None], looked, jnp.zeros_like(looked))
    rows = looked.reshape(fsdp_size, own_rows, width)
    mine = jnp.stack([*jnp.split(w_qkv, 3, axis=1), w_out])
    inputs, weights = prepare(rows, mine, deep)
    inputs, weights, centroids_t = lax.optimization_barrier((inputs, weights, centroids_t))
    cent = lax.all_to_all(centroids_t, "fsdp", split_axis=1, concat_axis=0, tiled=True)
    weights = weights.reshape(4, width, width)
    encoded = encode_quarters(inputs, weights, ln_gain, ln_bias)
    tokens = every_token(encoded, deep).reshape(-1, width)
    per_dev = cent.shape[1]
    base = (dp_rank * fsdp_size + fsdp_rank) * per_dev
    peak, mass, pick, new = owner(tokens, cent, assignments - base)
    stats = jnp.stack([peak, mass, pick]).reshape(3, dp_size * fsdp_size, own_rows).transpose(1, 0, 2)
    stats = lax.all_to_all(stats, ("dp", "fsdp"), split_axis=0, concat_axis=0, tiled=True)
    top = jnp.max(stats[:, 0], axis=0)
    total = jnp.sum(stats[:, 1] * jnp.exp(stats[:, 0] - top[None]), axis=0)
    return jnp.log(total) + top - jnp.sum(stats[:, 2], axis=0), new


def encode_quarters(inputs, weights, ln_gain, ln_bias):
    passages = inputs.shape[0] // SEQ

    def heads(q):
        part = jnp.dot(inputs, weights[q], preferred_element_type=jnp.float32).astype(jnp.bfloat16)
        return part.reshape(passages, SEQ, HEADS, HEAD)

    scores = jnp.einsum(
        "bqhd,bkhd->bhqk", heads(0), heads(1), preferred_element_type=jnp.float32
    ) * (1.0 / math.sqrt(HEAD))
    probs = jax.nn.softmax(scores, axis=-1).astype(jnp.bfloat16)
    context = jnp.einsum("bhqk,bkhd->bqhd", probs, heads(2), preferred_element_type=jnp.float32)
    context = context.astype(jnp.bfloat16).reshape(inputs.shape[0], HEADS * HEAD)
    mixed = jnp.dot(context, weights[3], preferred_element_type=jnp.float32) + inputs.astype(
        jnp.float32
    )
    return layer_norm(mixed, ln_gain, ln_bias).astype(jnp.bfloat16)


def plan(mesh):
    dp_size, fsdp_size = mesh.shape["dp"], mesh.shape["fsdp"]

    def either(*args):
        few_tokens = args[7].shape[0] <= args[6].shape[1]
        paired = dp_size == 4 and fsdp_size % 2 == 0
        return token_shards(*args) if few_tokens and paired else shards(*args)

    return either


def solution(mesh):
    return jax.shard_map(
        plan(mesh),
        mesh=mesh,
        in_specs=(
            P("dp"),
            P("fsdp", None),
            P("fsdp", None),
            P("fsdp", None),
            P(),
            P(),
            P("fsdp", "dp"),
            P(),
        ),
        out_specs=(P(("dp", "fsdp")), P(("dp", "fsdp"), None)),
        check_vma=False,
    )
```

```python
import functools
import math

import jax
import jax.numpy as jnp
from jax import lax
from jax.experimental import pallas as pl
from jax.experimental.pallas import tpu as pltpu
from jax.sharding import PartitionSpec as P

HEADS = 12
HEAD = 64
SEQ = 128


def joined(shard, axis, combine):
    everything = jax.tree.map(lambda part: lax.all_gather(part, axis), shard)
    initial = jax.tree.map(lambda part: part[0], everything)

    def lap(k, so_far):
        return combine(so_far, jax.tree.map(lambda part: part[k], everything))

    return lax.fori_loop(1, lax.axis_size(axis), lap, initial)


def layer_norm(values, ln_gain, ln_bias):
    center = values - jnp.mean(values, axis=-1, keepdims=True)
    spread = jnp.mean(center * center, axis=-1, keepdims=True)
    return center * lax.rsqrt(spread + 1e-05) * ln_gain + ln_bias


def encode(inputs, qkv_full, out_full, ln_gain, ln_bias):
    passages = inputs.shape[0] // SEQ
    packed = jnp.dot(inputs, qkv_full, preferred_element_type=jnp.float32).astype(jnp.bfloat16)
    packed = packed.reshape(passages, SEQ, 3, HEADS, HEAD)
    scores = jnp.einsum(
        "bqhd,bkhd->bhqk", packed[:, :, 0], packed[:, :, 1], preferred_element_type=jnp.float32
    ) * (1.0 / math.sqrt(HEAD))
    probs = jax.nn.softmax(scores, axis=-1).astype(jnp.bfloat16)
    context = jnp.einsum(
        "bhqk,bkhd->bqhd", probs, packed[:, :, 2], preferred_element_type=jnp.float32
    )
    context = context.astype(jnp.bfloat16).reshape(inputs.shape[0], HEADS * HEAD)
    mixed = jnp.dot(context, out_full, preferred_element_type=jnp.float32) + inputs.astype(
        jnp.float32
    )
    return layer_norm(mixed, ln_gain, ln_bias).astype(jnp.bfloat16)


def one_hot_sums(rows, targets, width):
    count = rows.shape[0]
    step_rows = math.gcd(count, 512)
    columns = jnp.arange(width, dtype=jnp.int32)

    def one_visit(totals, pieces):
        block_rows, block_targets = pieces
        hits = (block_targets[:, None] == columns[None, :]).astype(jnp.bfloat16)
        return (
            totals
            + lax.dot_general(
                hits, block_rows, (((0,), (0,)), ((), ())), preferred_element_type=jnp.float32
            ),
            None,
        )

    start = jnp.zeros((width, rows.shape[1]), jnp.float32)
    totals, unused = lax.scan(
        one_visit,
        start,
        (
            rows.reshape(count // step_rows, step_rows, rows.shape[1]),
            targets.reshape(count // step_rows, step_rows),
        ),
    )
    return totals


def combine_parts(first, second):
    peak = jnp.maximum(first[0], second[0])
    mass = first[1] * jnp.exp(first[0] - peak) + second[1] * jnp.exp(second[0] - peak)
    return (peak, mass, first[2] + second[2])


def shards(token_ids, embed_table, w_qkv, w_out, ln_gain, ln_bias, centroids_t, assignments):
    dp_size = lax.axis_size("dp")
    fsdp_size = lax.axis_size("fsdp")
    dp_rank = lax.axis_index("dp")
    fsdp_rank = lax.axis_index("fsdp")
    vocab_rows = embed_table.shape[0]
    local_ids = token_ids - fsdp_rank * vocab_rows
    inside = (local_ids >= 0) & (local_ids < vocab_rows)
    looked = jnp.take(embed_table, jnp.clip(local_ids, 0, vocab_rows - 1), axis=0)
    looked = jnp.where(inside[:, None], looked, jnp.zeros_like(looked))
    inputs = (
        lax.psum_scatter(looked, "fsdp", scatter_dimension=0, tiled=True)
        .astype(jnp.float32)
        .astype(jnp.bfloat16)
    )
    qkv_full, out_full, cent_full = (
        lax.all_gather(w_qkv, "fsdp", axis=0, tiled=True),
        lax.all_gather(w_out, "fsdp", axis=0, tiled=True),
        lax.all_gather(centroids_t, "fsdp", axis=0, tiled=True),
    )
    encoded = encode(inputs, qkv_full, out_full, ln_gain, ln_bias)
    own_rows = encoded.shape[0]
    width = encoded.shape[1]
    block_width = cent_full.shape[1]
    per_dev = block_width // fsdp_size
    slab = lax.all_gather(encoded, "dp", axis=0, tiled=True)
    slab_assign = lax.dynamic_index_in_dim(
        assignments.reshape(dp_size, fsdp_size, own_rows), fsdp_rank, 1, keepdims=False
    ).reshape(-1)
    owned = slab_assign - dp_rank * block_width
    slab_rows = slab.shape[0]
    step_rows = math.gcd(slab_rows, 512)
    columns = jnp.arange(block_width, dtype=jnp.int32)

    def body_visit(totals, pieces):
        block_rows, local = pieces
        logits = jnp.dot(block_rows, cent_full, preferred_element_type=jnp.float32)
        peak = jnp.max(logits, axis=1)
        mass = jnp.sum(jnp.exp(logits - peak[:, None]), axis=1)
        hits = local[:, None] == columns[None, :]
        picked = jnp.sum(jnp.where(hits, logits, 0.0), axis=1)
        return (totals, (peak, mass, picked))

    start = jnp.zeros((1,), jnp.float32)
    partial_value, stats = lax.scan(
        body_visit,
        start,
        (
            slab.reshape(slab_rows // step_rows, step_rows, width),
            owned.reshape(slab_rows // step_rows, step_rows),
        ),
    )
    peaks, masses, picks = (stats[0].reshape(-1), stats[1].reshape(-1), stats[2].reshape(-1))
    peaks, masses, picks = joined((peaks, masses, picks), "dp", combine_parts)
    peak_own = lax.dynamic_slice_in_dim(peaks, dp_rank * own_rows, own_rows)
    mass_own = lax.dynamic_slice_in_dim(masses, dp_rank * own_rows, own_rows)
    pick_own = lax.dynamic_slice_in_dim(picks, dp_rank * own_rows, own_rows)
    token_loss = jnp.log(mass_own) + peak_own - pick_own
    share = lax.all_to_all(encoded, "fsdp", split_axis=1, concat_axis=0, tiled=True)
    every_rows = lax.all_gather(share, "dp", axis=0, tiled=True)
    block_local = assignments - dp_rank * block_width
    partial_share = one_hot_sums(every_rows, block_local, block_width)
    totals = lax.all_to_all(partial_share, "fsdp", split_axis=0, concat_axis=1, tiled=True)
    base = dp_rank * block_width + fsdp_rank * per_dev
    targets = base + jnp.arange(per_dev, dtype=jnp.int32)
    counts = jnp.sum((assignments[:, None] == targets[None, :]).astype(jnp.int32), axis=0)
    previous = lax.dynamic_slice_in_dim(cent_full, fsdp_rank * per_dev, per_dev, 1).T.astype(
        jnp.float32
    )
    new_centroids = jnp.where(
        counts[:, None] > 0, totals / jnp.maximum(counts, 1)[:, None].astype(jnp.float32), previous
    )
    return (token_loss, new_centroids)


VMEM_LIMIT = 60 * 1024 * 1024
WHOLE_VMEM = pl.BlockSpec(memory_space=pltpu.VMEM)


class Place:
    def __init__(self, deep):
        self.deep = deep
        self.dp, self.fsdp = lax.axis_index("dp"), lax.axis_index("fsdp")
        self.x, self.c = self.dp // 2, self.dp % 2
        self.z, self.y = self.fsdp // 2, self.fsdp % 2

    def at(self, x=None, c=None, z=None, y=None):
        x, c = self.x if x is None else x, self.c if c is None else c
        z, y = self.z if z is None else z, self.y if y is None else y
        return {"dp": x * 2 + c, "fsdp": z * 2 + y}

    def greet(self):
        barrier = pltpu.get_barrier_semaphore()
        everyone = 8 * self.deep
        me = self.dp * 2 * self.deep + self.fsdp

        @pl.loop(1, everyone)
        def each(k):
            peer = (me + k) % everyone
            there = {"dp": peer // (2 * self.deep), "fsdp": peer % (2 * self.deep)}
            pl.semaphore_signal(barrier, inc=1, device_id=there, device_id_type=pl.DeviceIdType.MESH)

        pl.semaphore_wait(barrier, everyone - 1)


class Sender:
    def __init__(self, sems):
        self.sems, self.used, self.sent = sems, 0, []

    def send(self, src, dst, recv_sem, peer, when=None):
        copy = pltpu.make_async_remote_copy(
            src_ref=src,
            dst_ref=dst,
            send_sem=self.sems.at[self.used],
            recv_sem=recv_sem,
            device_id=peer,
            device_id_type=pl.DeviceIdType.MESH,
        )
        self.used += 1
        self.sent.append((copy, when))
        guarded(when, copy.start)

    def arrived(self, dst, recv_sem, peer, when=None):
        copy = pltpu.make_async_remote_copy(
            src_ref=dst,
            dst_ref=dst,
            send_sem=self.sems.at[0],
            recv_sem=recv_sem,
            device_id=peer,
            device_id_type=pl.DeviceIdType.MESH,
        )
        guarded(when, copy.wait_recv)

    def drain(self):
        for copy, when in self.sent:
            guarded(when, copy.wait_send)


def guarded(when, action):
    if when is None:
        action()
    else:
        pl.when(when)(action)


def near_first(z, k, deep):
    below, above = z, deep - 1 - z
    both = jnp.minimum(below, above)
    swing = z - (k + 1) // 2 if k % 2 else z + k // 2
    far = jnp.where(above > below, z + k - both, z - k + both)
    return jnp.where(k <= 2 * both, swing, far)


def passage(x, quarters, gain, bias, w_ref):
    width = x.shape[1]

    def dense(rows, q):
        weights = w_ref[q].reshape(width, width)
        return jnp.dot(rows, weights, preferred_element_type=jnp.float32)

    query, key, value = (dense(x, q).astype(jnp.bfloat16) for q in quarters[:3])
    context = []
    for head in range(HEADS):
        at = slice(head * HEAD, (head + 1) * HEAD)
        scores = lax.dot_general(
            query[:, at], key[:, at], (((1,), (1,)), ((), ())), preferred_element_type=jnp.float32
        ) * (1.0 / math.sqrt(HEAD))
        weight = jnp.exp(scores - jnp.max(scores, axis=1, keepdims=True))
        probs = (weight / jnp.sum(weight, axis=1, keepdims=True)).astype(jnp.bfloat16)
        context.append(jnp.dot(probs, value[:, at], preferred_element_type=jnp.float32))
    context = jnp.concatenate(context, axis=1).astype(jnp.bfloat16)
    mixed = dense(context, quarters[3]) + x.astype(jnp.float32)
    return layer_norm(mixed, gain, bias).astype(jnp.bfloat16)


def step_kernel(
    deep,
    ids_ref,
    table_ref,
    qkv_ref,
    out_w_ref,
    gain_ref,
    bias_ref,
    cent_ref,
    assign_ref,
    loss_ref,
    new_ref,
    rows,
    w,
    from_y,
    joined_y,
    from_z,
    cent,
    old,
    mine,
    tokens,
    counts,
    stat,
    got,
    load_sems,
    send_sems,
    y_sems,
    z_sems,
    w_sems,
    cent_sems,
    token_sems,
    stat_send,
    stat_recv,
):
    place = Place(deep)
    x, c, z, y = place.x, place.c, place.z, place.y
    own = place.fsdp
    parts = 2 * deep
    vocab_rows, width = table_ref.shape
    own_rows = mine.shape[0]
    per_dev = new_ref.shape[0]
    blocks = 4 * parts
    own_block = place.dp * parts + own
    quarter, across = x * 2 + c, (1 - x) * 2 + c
    partner, x_side, y_side = place.at(c=1 - c), place.at(x=1 - x), place.at(y=1 - y)
    up, down = place.at(z=jnp.minimum(z + 1, deep - 1)), place.at(z=jnp.maximum(z - 1, 0))

    loads = []
    for q in range(4):
        part = qkv_ref.at[:, pl.ds(q * width, width)] if q < 3 else out_w_ref
        loads.append(pltpu.make_async_copy(part, w.at[q, own], load_sems.at[q]))
    loads.append(
        pltpu.make_async_copy(
            cent_ref.at[:, pl.ds(pl.multiple_of(own * per_dev, 128), per_dev)], cent.at[own], load_sems.at[4]
        )
    )
    for load in loads:
        load.start()

    def look(block):
        local = ids_ref[block] - own * vocab_rows
        hot = local == lax.broadcasted_iota(jnp.int32, (own_rows, vocab_rows), 1)
        rows[block] = jnp.dot(
            jnp.where(hot, 1.0, 0.0).astype(jnp.bfloat16), table_ref[...], preferred_element_type=jnp.float32
        ).astype(jnp.bfloat16)

    look((z + 1) % deep * 2 + (1 - y))
    place.greet()
    out = Sender(send_sems)
    for load in loads:
        load.wait()

    home = w.at[quarter, own]
    out.send(home, home, w_sems.at[quarter, own], up, z + 1 < deep)
    out.send(home, home, w_sems.at[quarter, own], down, z > 0)
    for k in range(1, deep + 1):
        to = (z + k) % deep
        if k > 1:
            look(to * 2 + (1 - y))
        out.send(rows.at[to * 2 + (1 - y)], from_y.at[to], y_sems.at[to], y_side)
    for k in range(1, deep + 1):
        look((z + k) % deep * 2 + y)

    def spread(s):
        block = w.at[quarter, s]
        out.send(block, block, w_sems.at[quarter, s], x_side)
        out.send(block, block, w_sems.at[quarter, s], partner)

    def join(k):
        to = (z + k) % deep
        out.arrived(from_y.at[to], y_sems.at[to], y_side)
        joined_y[to] = from_y[to] + rows[to * 2 + y]
        if k < deep:
            out.send(joined_y.at[to], from_z.at[deep - k], z_sems.at[deep - k], place.at(z=to))

    for k in range(1, deep):
        z0 = near_first(z, k, deep)
        s = z0 * 2 + y
        block = w.at[quarter, s]
        out.arrived(block, w_sems.at[quarter, s], y_side)
        out.send(block, block, w_sems.at[quarter, s], up, (z0 < z) & (z + 1 < deep))
        out.send(block, block, w_sems.at[quarter, s], down, (z0 > z) & (z > 0))
        spread(s)
        join(k)
    join(deep)
    for k in range(deep):
        block = w.at[quarter, near_first(z, k, deep) * 2 + y]
        out.send(block, block, w_sems.at[quarter, near_first(z, k, deep) * 2 + y], y_side)
    for k in range(1, parts):
        to = (own + k) % parts
        columns = pl.ds(pl.multiple_of(to * per_dev, 128), per_dev)
        out.send(
            cent_ref.at[:, columns], cent.at[own], cent_sems.at[own], {"dp": place.dp, "fsdp": to}
        )
    for k in range(deep):
        s = near_first(z, k, deep) * 2 + (1 - y)
        out.arrived(w.at[quarter, s], w_sems.at[quarter, s], y_side)
        spread(s)
    others = [near_first(z, k, deep) * 2 + y for k in range(1, deep)]
    others += [near_first(z, k, deep) * 2 + (1 - y) for k in range(deep)]
    for s in others:
        block = w.at[across, s]
        out.arrived(block, w_sems.at[across, s], x_side)
        out.send(block, block, w_sems.at[across, s], partner)
    total = joined_y[z]
    for k in range(1, deep):
        out.arrived(from_z.at[k], z_sems.at[k], y_side)
        total = total + from_z[k]
    for q in (x * 2 + (1 - c), (1 - x) * 2 + (1 - c)):
        for s in others:
            out.arrived(w.at[q, s], w_sems.at[q, s], partner)
    for first in range(0, own_rows, SEQ):
        mine[pl.ds(first, SEQ), :] = passage(
            total[first : first + SEQ], range(4), gain_ref[...], bias_ref[...], w
        )

    x_first = c == 1
    second_xy = (jnp.where(x_first, 1 - x, x), jnp.where(x_first, y, 1 - y))
    third_xy = (jnp.where(x_first, x, 1 - x), jnp.where(x_first, 1 - y, y))
    second = place.at(x=second_xy[0], y=second_xy[1])
    third = place.at(x=third_xy[0], y=third_xy[1])

    def number(x0, c0, z0, y0):
        return ((x0 * 2 + c0) * deep + z0) * 2 + y0

    def push(b, peer, when=None, src=None):
        block = tokens.at[b]
        out.send(block if src is None else src, block, token_sems.at[b], peer, when)

    def wait(b):
        out.arrived(tokens.at[b], token_sems.at[b], partner)

    push(own_block, up, z + 1 < deep, mine)
    push(own_block, down, z > 0, mine)
    for peer in (second, third, partner):
        push(own_block, peer, None, mine)
    tokens[own_block] = mine[...]
    new_ref[...] = jnp.zeros_like(new_ref)
    counts[...] = jnp.zeros_like(counts)
    base = own_block * per_dev
    centroid = lax.broadcasted_iota(jnp.int32, (per_dev, 2 * own_rows), 0) + base

    def pair_of(p):
        hits = centroid == assign_ref[p]
        return hits, tokens[pl.ds(p * 2, 2)].reshape(2 * own_rows, width)

    def add_up(p):
        hits, some = pair_of(p)
        ones = jnp.where(hits, 1.0, 0.0)
        counts[...] += jnp.sum(ones, axis=1, keepdims=True)
        new_ref[...] += jnp.dot(
            ones.astype(jnp.bfloat16), some, preferred_element_type=jnp.float32
        )

    def score(p):
        hits, some = pair_of(p)
        logits = lax.dot_general(
            old[...], some, (((1,), (1,)), ((), ())), preferred_element_type=jnp.float32
        )
        peak = jnp.max(logits, axis=0, keepdims=True)
        mass = jnp.sum(jnp.exp(logits - peak), axis=0, keepdims=True)
        pick = jnp.sum(jnp.where(hits, logits, 0.0), axis=0, keepdims=True)
        for half in range(2):
            b = p * 2 + half
            at = slice(half * own_rows, (half + 1) * own_rows)
            for k, row in enumerate((peak, mass, pick)):
                stat[b, pl.ds(k, 1), :] = row[:, at]
            pl.when(b != own_block)(stat_copy(b).start)

    def stat_copy(b):
        return pltpu.make_async_remote_copy(
            src_ref=stat.at[b],
            dst_ref=got.at[own_block],
            send_sem=stat_send.at[b],
            recv_sem=stat_recv.at[own_block],
            device_id={"dp": b // parts, "fsdp": b % parts},
            device_id_type=pl.DeviceIdType.MESH,
        )

    def finish_line(z1):
        for xx, yy in (third_xy, (1 - x, 1 - y)):
            b = number(xx, c, z1, yy)
            wait(b)
            push(b, partner)

    def sums_of(z1):
        for x0 in range(2):
            for y0 in range(2):
                wait(number(x0, 1 - c, z1, y0))

        @pl.loop(0, 4)
        def each(i):
            add_up(i * deep + z1)

    for k in range(deep):
        z0 = near_first(z, k, deep)
        if k > 0:
            b = number(x, c, z0, y)
            wait(b)
            push(b, up, (z0 < z) & (z + 1 < deep))
            push(b, down, (z0 > z) & (z > 0))
            push(b, second)
            push(b, third)
            push(b, partner)
        b = number(second_xy[0], c, z0, second_xy[1])
        wait(b)
        push(b, third)
        push(b, partner)
        if k >= 1:
            finish_line(near_first(z, k - 1, deep))
        if k >= 2:
            sums_of(near_first(z, k - 2, deep))
    finish_line(near_first(z, deep - 1, deep))
    for k in range(1, parts):
        s = (own + k) % parts
        out.arrived(cent.at[s], cent_sems.at[s], partner)
    old[...] = cent[...].reshape(width, per_dev).T
    for k in range(max(deep - 2, 0), deep):
        sums_of(near_first(z, k, deep))

    @pl.loop(0, 4 * deep)
    def each(p):
        score(p)

    many = counts[...]
    new_ref[...] = jnp.where(
        many > 0, new_ref[...] / jnp.maximum(many, 1.0), old[...].astype(jnp.float32)
    )
    got[own_block] = stat[own_block]

    @pl.loop(0, blocks)
    def each_device(b):
        @pl.when(b != own_block)
        def done():
            stat_copy(b).wait_send()
            pltpu.make_async_remote_copy(
                src_ref=got.at[b],
                dst_ref=got.at[b],
                send_sem=stat_send.at[b],
                recv_sem=stat_recv.at[b],
                device_id=partner,
                device_id_type=pl.DeviceIdType.MESH,
            ).wait_recv()

    peaks, masses, picks = (got[:, k, :] for k in range(3))
    top = jnp.max(peaks, axis=0, keepdims=True)
    mass = jnp.sum(masses * jnp.exp(peaks - top), axis=0, keepdims=True)
    loss_ref[...] = jnp.log(mass) + top - jnp.sum(picks, axis=0, keepdims=True)
    out.drain()


def token_shards(token_ids, embed_table, w_qkv, w_out, ln_gain, ln_bias, centroids_t, assignments):
    parts = lax.axis_size("fsdp")
    deep = parts // 2
    blocks = 4 * parts
    width = embed_table.shape[1]
    feats = w_qkv.shape[0]
    own_rows = token_ids.shape[0] // parts
    per_dev = centroids_t.shape[1] // parts
    half = jnp.bfloat16
    block = (own_rows, width)
    sems = pltpu.SemaphoreType.DMA
    loss, new = pl.pallas_call(
        functools.partial(step_kernel, deep),
        out_shape=(
            jax.ShapeDtypeStruct((1, own_rows), jnp.float32),
            jax.ShapeDtypeStruct((per_dev, width), jnp.float32),
        ),
        in_specs=[
            WHOLE_VMEM,
            WHOLE_VMEM,
            WHOLE_VMEM,
            WHOLE_VMEM,
            WHOLE_VMEM,
            WHOLE_VMEM,
            pl.BlockSpec(memory_space=pl.ANY),
            WHOLE_VMEM,
        ],
        out_specs=(WHOLE_VMEM, WHOLE_VMEM),
        scratch_shapes=[
            pltpu.VMEM((parts, *block), half),
            pltpu.VMEM((4, parts, feats, width), half),
            pltpu.VMEM((deep, *block), half),
            pltpu.VMEM((deep, *block), half),
            pltpu.VMEM((deep, *block), half),
            pltpu.VMEM((parts, feats, per_dev), half),
            pltpu.VMEM((per_dev, width), half),
            pltpu.VMEM(block, half),
            pltpu.VMEM((blocks, *block), half),
            pltpu.VMEM((per_dev, 1), jnp.float32),
            pltpu.VMEM((blocks, 8, own_rows), jnp.float32),
            pltpu.VMEM((blocks, 8, own_rows), jnp.float32),
            sems((5,)),
            sems((64 * deep,)),
            sems((deep,)),
            sems((deep,)),
            sems((4, parts)),
            sems((parts,)),
            sems((blocks,)),
            sems((blocks,)),
            sems((blocks,)),
        ],
        compiler_params=pltpu.CompilerParams(
            collective_id=0, has_side_effects=True, vmem_limit_bytes=VMEM_LIMIT
        ),
        name="whole_step",
    )(
        token_ids.reshape(parts, own_rows, 1),
        embed_table,
        w_qkv,
        w_out,
        ln_gain[None],
        ln_bias[None],
        centroids_t,
        assignments.reshape(blocks // 2, 1, 2 * own_rows),
    )
    return loss.reshape(own_rows), new


def plan(mesh):
    dp_size, fsdp_size = mesh.shape["dp"], mesh.shape["fsdp"]

    def either(*args):
        few_tokens = args[7].shape[0] <= args[6].shape[1]
        paired = dp_size == 4 and fsdp_size % 2 == 0
        return token_shards(*args) if few_tokens and paired else shards(*args)

    return either


def solution(mesh):
    return jax.shard_map(
        plan(mesh),
        mesh=mesh,
        in_specs=(
            P("dp"),
            P("fsdp", None),
            P("fsdp", None),
            P("fsdp", None),
            P(),
            P(),
            P("fsdp", "dp"),
            P(),
        ),
        out_specs=(P(("dp", "fsdp")), P(("dp", "fsdp"), None)),
        check_vma=False,
    )
```

```python
import functools
import math

import jax
import jax.numpy as jnp
from jax import lax
from jax.experimental import pallas as pl
from jax.experimental.pallas import tpu as pltpu
from jax.sharding import PartitionSpec as P

HEADS = 12
HEAD = 64
SEQ = 128


def joined(shard, axis, combine):
    everything = jax.tree.map(lambda part: lax.all_gather(part, axis), shard)
    initial = jax.tree.map(lambda part: part[0], everything)

    def lap(k, so_far):
        return combine(so_far, jax.tree.map(lambda part: part[k], everything))

    return lax.fori_loop(1, lax.axis_size(axis), lap, initial)


def layer_norm(values, ln_gain, ln_bias):
    center = values - jnp.mean(values, axis=-1, keepdims=True)
    spread = jnp.mean(center * center, axis=-1, keepdims=True)
    return center * lax.rsqrt(spread + 1e-05) * ln_gain + ln_bias


def encode(inputs, qkv_full, out_full, ln_gain, ln_bias):
    passages = inputs.shape[0] // SEQ
    packed = jnp.dot(inputs, qkv_full, preferred_element_type=jnp.float32).astype(jnp.bfloat16)
    packed = packed.reshape(passages, SEQ, 3, HEADS, HEAD)
    scores = jnp.einsum(
        "bqhd,bkhd->bhqk", packed[:, :, 0], packed[:, :, 1], preferred_element_type=jnp.float32
    ) * (1.0 / math.sqrt(HEAD))
    probs = jax.nn.softmax(scores, axis=-1).astype(jnp.bfloat16)
    context = jnp.einsum(
        "bhqk,bkhd->bqhd", probs, packed[:, :, 2], preferred_element_type=jnp.float32
    )
    context = context.astype(jnp.bfloat16).reshape(inputs.shape[0], HEADS * HEAD)
    mixed = jnp.dot(context, out_full, preferred_element_type=jnp.float32) + inputs.astype(
        jnp.float32
    )
    return layer_norm(mixed, ln_gain, ln_bias).astype(jnp.bfloat16)


def one_hot_sums(rows, targets, width):
    count = rows.shape[0]
    step_rows = math.gcd(count, 512)
    columns = jnp.arange(width, dtype=jnp.int32)

    def one_visit(totals, pieces):
        block_rows, block_targets = pieces
        hits = (block_targets[:, None] == columns[None, :]).astype(jnp.bfloat16)
        return (
            totals
            + lax.dot_general(
                hits, block_rows, (((0,), (0,)), ((), ())), preferred_element_type=jnp.float32
            ),
            None,
        )

    start = jnp.zeros((width, rows.shape[1]), jnp.float32)
    totals, unused = lax.scan(
        one_visit,
        start,
        (
            rows.reshape(count // step_rows, step_rows, rows.shape[1]),
            targets.reshape(count // step_rows, step_rows),
        ),
    )
    return totals


def combine_parts(first, second):
    peak = jnp.maximum(first[0], second[0])
    mass = first[1] * jnp.exp(first[0] - peak) + second[1] * jnp.exp(second[0] - peak)
    return (peak, mass, first[2] + second[2])


def shards(token_ids, embed_table, w_qkv, w_out, ln_gain, ln_bias, centroids_t, assignments):
    dp_size = lax.axis_size("dp")
    fsdp_size = lax.axis_size("fsdp")
    dp_rank = lax.axis_index("dp")
    fsdp_rank = lax.axis_index("fsdp")
    vocab_rows = embed_table.shape[0]
    local_ids = token_ids - fsdp_rank * vocab_rows
    inside = (local_ids >= 0) & (local_ids < vocab_rows)
    looked = jnp.take(embed_table, jnp.clip(local_ids, 0, vocab_rows - 1), axis=0)
    looked = jnp.where(inside[:, None], looked, jnp.zeros_like(looked))
    inputs = (
        lax.psum_scatter(looked, "fsdp", scatter_dimension=0, tiled=True)
        .astype(jnp.float32)
        .astype(jnp.bfloat16)
    )
    qkv_full, out_full, cent_full = (
        lax.all_gather(w_qkv, "fsdp", axis=0, tiled=True),
        lax.all_gather(w_out, "fsdp", axis=0, tiled=True),
        lax.all_gather(centroids_t, "fsdp", axis=0, tiled=True),
    )
    encoded = encode(inputs, qkv_full, out_full, ln_gain, ln_bias)
    own_rows = encoded.shape[0]
    width = encoded.shape[1]
    block_width = cent_full.shape[1]
    per_dev = block_width // fsdp_size
    slab = lax.all_gather(encoded, "dp", axis=0, tiled=True)
    slab_assign = lax.dynamic_index_in_dim(
        assignments.reshape(dp_size, fsdp_size, own_rows), fsdp_rank, 1, keepdims=False
    ).reshape(-1)
    owned = slab_assign - dp_rank * block_width
    slab_rows = slab.shape[0]
    step_rows = math.gcd(slab_rows, 512)
    columns = jnp.arange(block_width, dtype=jnp.int32)

    def body_visit(totals, pieces):
        block_rows, local = pieces
        logits = jnp.dot(block_rows, cent_full, preferred_element_type=jnp.float32)
        peak = jnp.max(logits, axis=1)
        mass = jnp.sum(jnp.exp(logits - peak[:, None]), axis=1)
        hits = local[:, None] == columns[None, :]
        picked = jnp.sum(jnp.where(hits, logits, 0.0), axis=1)
        return (totals, (peak, mass, picked))

    start = jnp.zeros((1,), jnp.float32)
    partial_value, stats = lax.scan(
        body_visit,
        start,
        (
            slab.reshape(slab_rows // step_rows, step_rows, width),
            owned.reshape(slab_rows // step_rows, step_rows),
        ),
    )
    peaks, masses, picks = (stats[0].reshape(-1), stats[1].reshape(-1), stats[2].reshape(-1))
    peaks, masses, picks = joined((peaks, masses, picks), "dp", combine_parts)
    peak_own = lax.dynamic_slice_in_dim(peaks, dp_rank * own_rows, own_rows)
    mass_own = lax.dynamic_slice_in_dim(masses, dp_rank * own_rows, own_rows)
    pick_own = lax.dynamic_slice_in_dim(picks, dp_rank * own_rows, own_rows)
    token_loss = jnp.log(mass_own) + peak_own - pick_own
    share = lax.all_to_all(encoded, "fsdp", split_axis=1, concat_axis=0, tiled=True)
    every_rows = lax.all_gather(share, "dp", axis=0, tiled=True)
    block_local = assignments - dp_rank * block_width
    partial_share = one_hot_sums(every_rows, block_local, block_width)
    totals = lax.all_to_all(partial_share, "fsdp", split_axis=0, concat_axis=1, tiled=True)
    base = dp_rank * block_width + fsdp_rank * per_dev
    targets = base + jnp.arange(per_dev, dtype=jnp.int32)
    counts = jnp.sum((assignments[:, None] == targets[None, :]).astype(jnp.int32), axis=0)
    previous = lax.dynamic_slice_in_dim(cent_full, fsdp_rank * per_dev, per_dev, 1).T.astype(
        jnp.float32
    )
    new_centroids = jnp.where(
        counts[:, None] > 0, totals / jnp.maximum(counts, 1)[:, None].astype(jnp.float32), previous
    )
    return (token_loss, new_centroids)


VMEM_LIMIT = 60 * 1024 * 1024
WHOLE_VMEM = pl.BlockSpec(memory_space=pltpu.VMEM)


class Place:
    def __init__(self, deep):
        self.deep = deep
        self.dp, self.fsdp = lax.axis_index("dp"), lax.axis_index("fsdp")
        self.x, self.c = self.dp // 2, self.dp % 2
        self.z, self.y = self.fsdp // 2, self.fsdp % 2

    def at(self, x=None, c=None, z=None, y=None):
        x, c = self.x if x is None else x, self.c if c is None else c
        z, y = self.z if z is None else z, self.y if y is None else y
        return {"dp": x * 2 + c, "fsdp": z * 2 + y}

    def greet(self):
        barrier = pltpu.get_barrier_semaphore()
        everyone = 8 * self.deep
        me = self.dp * 2 * self.deep + self.fsdp

        @pl.loop(1, everyone)
        def each(k):
            peer = (me + k) % everyone
            there = {"dp": peer // (2 * self.deep), "fsdp": peer % (2 * self.deep)}
            pl.semaphore_signal(barrier, inc=1, device_id=there, device_id_type=pl.DeviceIdType.MESH)

        pl.semaphore_wait(barrier, everyone - 1)


class Sender:
    def __init__(self, sems):
        self.sems, self.used, self.sent = sems, 0, []

    def send(self, src, dst, recv_sem, peer, when=None):
        copy = pltpu.make_async_remote_copy(
            src_ref=src,
            dst_ref=dst,
            send_sem=self.sems.at[self.used],
            recv_sem=recv_sem,
            device_id=peer,
            device_id_type=pl.DeviceIdType.MESH,
        )
        self.used += 1
        self.sent.append((copy, when))
        guarded(when, copy.start)

    def arrived(self, dst, recv_sem, peer, when=None):
        copy = pltpu.make_async_remote_copy(
            src_ref=dst,
            dst_ref=dst,
            send_sem=self.sems.at[0],
            recv_sem=recv_sem,
            device_id=peer,
            device_id_type=pl.DeviceIdType.MESH,
        )
        guarded(when, copy.wait_recv)

    def drain(self):
        for copy, when in self.sent:
            guarded(when, copy.wait_send)


def guarded(when, action):
    if when is None:
        action()
    else:
        pl.when(when)(action)


def near_first(z, k, deep):
    below, above = z, deep - 1 - z
    both = jnp.minimum(below, above)
    swing = z - (k + 1) // 2 if k % 2 else z + k // 2
    far = jnp.where(above > below, z + k - both, z - k + both)
    return jnp.where(k <= 2 * both, swing, far)


def passage(x, quarters, gain, bias, w_ref):
    width = x.shape[1]

    def dense(rows, q):
        weights = w_ref[q].reshape(width, width)
        return jnp.dot(rows, weights, preferred_element_type=jnp.float32)

    query, key, value = (dense(x, q).astype(jnp.bfloat16) for q in quarters[:3])
    context = []
    for head in range(HEADS):
        at = slice(head * HEAD, (head + 1) * HEAD)
        scores = lax.dot_general(
            query[:, at], key[:, at], (((1,), (1,)), ((), ())), preferred_element_type=jnp.float32
        ) * (1.0 / math.sqrt(HEAD))
        weight = jnp.exp(scores - jnp.max(scores, axis=1, keepdims=True))
        probs = (weight / jnp.sum(weight, axis=1, keepdims=True)).astype(jnp.bfloat16)
        context.append(jnp.dot(probs, value[:, at], preferred_element_type=jnp.float32))
    context = jnp.concatenate(context, axis=1).astype(jnp.bfloat16)
    mixed = dense(context, quarters[3]) + x.astype(jnp.float32)
    return layer_norm(mixed, gain, bias).astype(jnp.bfloat16)


def step_kernel(
    deep,
    ids_ref,
    table_ref,
    qkv_ref,
    out_w_ref,
    norm_ref,
    cent_ref,
    assign_ref,
    loss_ref,
    new_ref,
    rows,
    w,
    from_y,
    joined_y,
    from_z,
    cent,
    old,
    mine,
    tokens,
    counts,
    stat,
    got,
    load_sems,
    send_sems,
    y_sems,
    z_sems,
    w_sems,
    cent_sems,
    token_sems,
    stat_send,
    stat_recv,
):
    place = Place(deep)
    x, c, z, y = place.x, place.c, place.z, place.y
    own = place.fsdp
    parts = 2 * deep
    vocab_rows, width = table_ref.shape
    own_rows = mine.shape[0]
    per_dev = new_ref.shape[0]
    blocks = 4 * parts
    own_block = place.dp * parts + own
    quarter, across = x * 2 + c, (1 - x) * 2 + c
    partner, x_side, y_side = place.at(c=1 - c), place.at(x=1 - x), place.at(y=1 - y)
    up, down = place.at(z=jnp.minimum(z + 1, deep - 1)), place.at(z=jnp.maximum(z - 1, 0))

    loads = []
    for q in range(4):
        part = qkv_ref.at[:, pl.ds(q * width, width)] if q < 3 else out_w_ref
        loads.append(pltpu.make_async_copy(part, w.at[q, own], load_sems.at[q]))
    loads.append(
        pltpu.make_async_copy(
            cent_ref.at[:, pl.ds(pl.multiple_of(own * per_dev, 128), per_dev)], cent.at[own], load_sems.at[4]
        )
    )
    for load in loads:
        load.start()

    def look(y0):
        local = ids_ref[y0] - own * vocab_rows
        hot = local == lax.broadcasted_iota(jnp.int32, (deep * own_rows, vocab_rows), 1)
        found = jnp.dot(
            jnp.where(hot, 1.0, 0.0).astype(jnp.bfloat16), table_ref[...], preferred_element_type=jnp.float32
        )
        rows[y0] = found.astype(jnp.bfloat16).reshape(deep, own_rows, width)

    place.greet()
    out = Sender(send_sems)
    for load in loads:
        load.wait()

    home = w.at[quarter, own]
    out.send(home, home, w_sems.at[quarter, own], up, z + 1 < deep)
    out.send(home, home, w_sems.at[quarter, own], down, z > 0)
    for k in range(1, deep + 1):
        to = (z + k) % deep
        if k == 1:
            look(1 - y)
        out.send(rows.at[1 - y, to], from_y.at[to], y_sems.at[to], y_side)
    look(y)

    def spread(s):
        block = w.at[quarter, s]
        out.send(block, block, w_sems.at[quarter, s], x_side)
        out.send(block, block, w_sems.at[quarter, s], partner)

    def join(k):
        to = (z + k) % deep
        out.arrived(from_y.at[to], y_sems.at[to], y_side)
        joined_y[to] = from_y[to] + rows[y, to]
        if k < deep:
            out.send(joined_y.at[to], from_z.at[deep - k], z_sems.at[deep - k], place.at(z=to))

    for k in range(1, deep):
        z0 = near_first(z, k, deep)
        s = z0 * 2 + y
        block = w.at[quarter, s]
        out.arrived(block, w_sems.at[quarter, s], y_side)
        out.send(block, block, w_sems.at[quarter, s], up, (z0 < z) & (z + 1 < deep))
        out.send(block, block, w_sems.at[quarter, s], down, (z0 > z) & (z > 0))
        spread(s)
    for k in range(1, deep + 1):
        join(k)
    for k in range(deep):
        block = w.at[quarter, near_first(z, k, deep) * 2 + y]
        out.send(block, block, w_sems.at[quarter, near_first(z, k, deep) * 2 + y], y_side)

    def give(z0, y0):
        to = z0 * 2 + y0
        columns = pl.ds(pl.multiple_of(to * per_dev, 128), per_dev)
        out.send(
            cent_ref.at[:, columns], cent.at[own], cent_sems.at[own], {"dp": place.dp, "fsdp": to}
        )

    for k in range(1, deep):
        give((z + k) % deep, y)
    for k in range(deep):
        s = near_first(z, k, deep) * 2 + (1 - y)
        out.arrived(w.at[quarter, s], w_sems.at[quarter, s], y_side)
        spread(s)
    for k in range(deep):
        give((z + k) % deep, 1 - y)
    others = [near_first(z, k, deep) * 2 + y for k in range(1, deep)]
    others += [near_first(z, k, deep) * 2 + (1 - y) for k in range(deep)]
    for s in others:
        block = w.at[across, s]
        out.arrived(block, w_sems.at[across, s], x_side)
        out.send(block, block, w_sems.at[across, s], partner)
    total = joined_y[z]
    for k in range(1, deep):
        out.arrived(from_z.at[k], z_sems.at[k], y_side)
        total = total + from_z[k]
    for q in (x * 2 + (1 - c), (1 - x) * 2 + (1 - c)):
        for s in others:
            out.arrived(w.at[q, s], w_sems.at[q, s], partner)
    for first in range(0, own_rows, SEQ):
        mine[pl.ds(first, SEQ), :] = passage(
            total[first : first + SEQ], range(4), norm_ref[0:1, :], norm_ref[1:2, :], w
        )

    x_first = c == 1
    second_xy = (jnp.where(x_first, 1 - x, x), jnp.where(x_first, y, 1 - y))
    third_xy = (jnp.where(x_first, x, 1 - x), jnp.where(x_first, 1 - y, y))
    second = place.at(x=second_xy[0], y=second_xy[1])
    third = place.at(x=third_xy[0], y=third_xy[1])

    def number(x0, c0, z0, y0):
        return ((x0 * 2 + c0) * deep + z0) * 2 + y0

    def push(b, peer, when=None, src=None):
        block = tokens.at[b]
        out.send(block if src is None else src, block, token_sems.at[b], peer, when)

    def wait(b):
        out.arrived(tokens.at[b], token_sems.at[b], partner)

    push(own_block, up, z + 1 < deep, mine)
    push(own_block, down, z > 0, mine)
    for peer in (second, third, partner):
        push(own_block, peer, None, mine)
    tokens[own_block] = mine[...]
    new_ref[...] = jnp.zeros_like(new_ref)
    counts[...] = jnp.zeros_like(counts)
    base = own_block * per_dev
    centroid = lax.broadcasted_iota(jnp.int32, (per_dev, 2 * own_rows), 0) + base

    def pair_of(p):
        hits = centroid == assign_ref[p]
        return hits, tokens[pl.ds(p * 2, 2)].reshape(2 * own_rows, width)

    def add_up(p):
        hits, some = pair_of(p)
        ones = jnp.where(hits, 1.0, 0.0)
        counts[...] += jnp.sum(ones, axis=1, keepdims=True)
        new_ref[...] += jnp.dot(
            ones.astype(jnp.bfloat16), some, preferred_element_type=jnp.float32
        )

    def score(p):
        hits, some = pair_of(p)
        logits = lax.dot_general(
            old[...], some, (((1,), (1,)), ((), ())), preferred_element_type=jnp.float32
        )
        peak = jnp.max(logits, axis=0, keepdims=True)
        mass = jnp.sum(jnp.exp(logits - peak), axis=0, keepdims=True)
        pick = jnp.sum(jnp.where(hits, logits, 0.0), axis=0, keepdims=True)
        for half in range(2):
            b = p * 2 + half
            at = slice(half * own_rows, (half + 1) * own_rows)
            for k, row in enumerate((peak, mass, pick)):
                stat[b, pl.ds(k, 1), :] = row[:, at]
            pl.when(b != own_block)(stat_copy(b).start)

    def stat_copy(b):
        return pltpu.make_async_remote_copy(
            src_ref=stat.at[b],
            dst_ref=got.at[own_block],
            send_sem=stat_send.at[b],
            recv_sem=stat_recv.at[own_block],
            device_id={"dp": b // parts, "fsdp": b % parts},
            device_id_type=pl.DeviceIdType.MESH,
        )

    def take_centroids():
        for k in range(1, parts):
            s = (own + k) % parts
            out.arrived(cent.at[s], cent_sems.at[s], partner)
        old[...] = cent[...].reshape(width, per_dev).T

    def finish_line(z1):
        for xx, yy in (third_xy, (1 - x, 1 - y)):
            b = number(xx, c, z1, yy)
            wait(b)
            push(b, partner)

    def sums_of(z1, with_scores):
        for x0 in range(2):
            for y0 in range(2):
                wait(number(x0, 1 - c, z1, y0))

        @pl.loop(0, 4)
        def each(i):
            add_up(i * deep + z1)
            if with_scores:
                score(i * deep + z1)

    for k in range(deep):
        z0 = near_first(z, k, deep)
        if k > 0:
            b = number(x, c, z0, y)
            wait(b)
            push(b, up, (z0 < z) & (z + 1 < deep))
            push(b, down, (z0 > z) & (z > 0))
            push(b, second)
            push(b, third)
            push(b, partner)
        b = number(second_xy[0], c, z0, second_xy[1])
        wait(b)
        push(b, third)
        push(b, partner)
        if k >= 1:
            finish_line(near_first(z, k - 1, deep))
        if k == deep - 2:
            take_centroids()
        if k >= 2:
            sums_of(near_first(z, k - 2, deep), True)
    finish_line(near_first(z, deep - 1, deep))
    for k in range(deep - 2, deep):
        sums_of(near_first(z, k, deep), True)

    many = counts[...]
    new_ref[...] = jnp.where(
        many > 0, new_ref[...] / jnp.maximum(many, 1.0), old[...].astype(jnp.float32)
    )
    got[own_block] = stat[own_block]

    @pl.loop(0, blocks)
    def each_device(b):
        @pl.when(b != own_block)
        def done():
            stat_copy(b).wait_send()
            pltpu.make_async_remote_copy(
                src_ref=got.at[b],
                dst_ref=got.at[b],
                send_sem=stat_send.at[b],
                recv_sem=stat_recv.at[b],
                device_id=partner,
                device_id_type=pl.DeviceIdType.MESH,
            ).wait_recv()

    peaks, masses, picks = (got[:, k, :] for k in range(3))
    top = jnp.max(peaks, axis=0, keepdims=True)
    mass = jnp.sum(masses * jnp.exp(peaks - top), axis=0, keepdims=True)
    loss_ref[...] = jnp.log(mass) + top - jnp.sum(picks, axis=0, keepdims=True)
    out.drain()


def token_shards(token_ids, embed_table, w_qkv, w_out, ln_gain, ln_bias, centroids_t, assignments):
    parts = lax.axis_size("fsdp")
    deep = parts // 2
    blocks = 4 * parts
    width = embed_table.shape[1]
    feats = w_qkv.shape[0]
    own_rows = token_ids.shape[0] // parts
    per_dev = centroids_t.shape[1] // parts
    half = jnp.bfloat16
    block = (own_rows, width)
    sems = pltpu.SemaphoreType.DMA
    loss, new = pl.pallas_call(
        functools.partial(step_kernel, deep),
        out_shape=(
            jax.ShapeDtypeStruct((1, own_rows), jnp.float32),
            jax.ShapeDtypeStruct((per_dev, width), jnp.float32),
        ),
        in_specs=[
            WHOLE_VMEM,
            WHOLE_VMEM,
            WHOLE_VMEM,
            WHOLE_VMEM,
            WHOLE_VMEM,
            pl.BlockSpec(memory_space=pl.ANY),
            WHOLE_VMEM,
        ],
        out_specs=(WHOLE_VMEM, WHOLE_VMEM),
        scratch_shapes=[
            pltpu.VMEM((2, deep, *block), half),
            pltpu.VMEM((4, parts, feats, width), half),
            pltpu.VMEM((deep, *block), half),
            pltpu.VMEM((deep, *block), half),
            pltpu.VMEM((deep, *block), half),
            pltpu.VMEM((parts, feats, per_dev), half),
            pltpu.VMEM((per_dev, width), half),
            pltpu.VMEM(block, half),
            pltpu.VMEM((blocks, *block), half),
            pltpu.VMEM((per_dev, 1), jnp.float32),
            pltpu.VMEM((blocks, 8, own_rows), jnp.float32),
            pltpu.VMEM((blocks, 8, own_rows), jnp.float32),
            sems((5,)),
            sems((64 * deep,)),
            sems((deep,)),
            sems((deep,)),
            sems((4, parts)),
            sems((parts,)),
            sems((blocks,)),
            sems((blocks,)),
            sems((blocks,)),
        ],
        compiler_params=pltpu.CompilerParams(
            collective_id=0, has_side_effects=True, vmem_limit_bytes=VMEM_LIMIT
        ),
        name="whole_step",
    )(
        token_ids.reshape(deep, 2, own_rows).transpose(1, 0, 2).reshape(2, deep * own_rows, 1),
        embed_table,
        w_qkv,
        w_out,
        jnp.stack([ln_gain, ln_bias]),
        centroids_t,
        assignments.reshape(blocks // 2, 1, 2 * own_rows),
    )
    return loss.reshape(own_rows), new


def plan(mesh):
    dp_size, fsdp_size = mesh.shape["dp"], mesh.shape["fsdp"]

    def either(*args):
        few_tokens = args[7].shape[0] <= args[6].shape[1]
        paired = dp_size == 4 and fsdp_size % 2 == 0
        return token_shards(*args) if few_tokens and paired else shards(*args)

    return either


def solution(mesh):
    return jax.shard_map(
        plan(mesh),
        mesh=mesh,
        in_specs=(
            P("dp"),
            P("fsdp", None),
            P("fsdp", None),
            P("fsdp", None),
            P(),
            P(),
            P("fsdp", "dp"),
            P(),
        ),
        out_specs=(P(("dp", "fsdp")), P(("dp", "fsdp"), None)),
        check_vma=False,
    )
```

```python
import functools
import math

import jax
import jax.numpy as jnp
from jax import lax
from jax.experimental import pallas as pl
from jax.experimental.pallas import tpu as pltpu
from jax.sharding import PartitionSpec as P

HEADS = 12
HEAD = 64
SEQ = 128


def joined(shard, axis, combine):
    everything = jax.tree.map(lambda part: lax.all_gather(part, axis), shard)
    initial = jax.tree.map(lambda part: part[0], everything)

    def lap(k, so_far):
        return combine(so_far, jax.tree.map(lambda part: part[k], everything))

    return lax.fori_loop(1, lax.axis_size(axis), lap, initial)


def layer_norm(values, ln_gain, ln_bias):
    center = values - jnp.mean(values, axis=-1, keepdims=True)
    spread = jnp.mean(center * center, axis=-1, keepdims=True)
    return center * lax.rsqrt(spread + 1e-05) * ln_gain + ln_bias


def encode(inputs, qkv_full, out_full, ln_gain, ln_bias):
    passages = inputs.shape[0] // SEQ
    packed = jnp.dot(inputs, qkv_full, preferred_element_type=jnp.float32).astype(jnp.bfloat16)
    packed = packed.reshape(passages, SEQ, 3, HEADS, HEAD)
    scores = jnp.einsum(
        "bqhd,bkhd->bhqk", packed[:, :, 0], packed[:, :, 1], preferred_element_type=jnp.float32
    ) * (1.0 / math.sqrt(HEAD))
    probs = jax.nn.softmax(scores, axis=-1).astype(jnp.bfloat16)
    context = jnp.einsum(
        "bhqk,bkhd->bqhd", probs, packed[:, :, 2], preferred_element_type=jnp.float32
    )
    context = context.astype(jnp.bfloat16).reshape(inputs.shape[0], HEADS * HEAD)
    mixed = jnp.dot(context, out_full, preferred_element_type=jnp.float32) + inputs.astype(
        jnp.float32
    )
    return layer_norm(mixed, ln_gain, ln_bias).astype(jnp.bfloat16)


def one_hot_sums(rows, targets, width):
    count = rows.shape[0]
    step_rows = math.gcd(count, 512)
    columns = jnp.arange(width, dtype=jnp.int32)

    def one_visit(totals, pieces):
        block_rows, block_targets = pieces
        hits = (block_targets[:, None] == columns[None, :]).astype(jnp.bfloat16)
        return (
            totals
            + lax.dot_general(
                hits, block_rows, (((0,), (0,)), ((), ())), preferred_element_type=jnp.float32
            ),
            None,
        )

    start = jnp.zeros((width, rows.shape[1]), jnp.float32)
    totals, unused = lax.scan(
        one_visit,
        start,
        (
            rows.reshape(count // step_rows, step_rows, rows.shape[1]),
            targets.reshape(count // step_rows, step_rows),
        ),
    )
    return totals


def combine_parts(first, second):
    peak = jnp.maximum(first[0], second[0])
    mass = first[1] * jnp.exp(first[0] - peak) + second[1] * jnp.exp(second[0] - peak)
    return (peak, mass, first[2] + second[2])


def shards(token_ids, embed_table, w_qkv, w_out, ln_gain, ln_bias, centroids_t, assignments):
    dp_size = lax.axis_size("dp")
    fsdp_size = lax.axis_size("fsdp")
    dp_rank = lax.axis_index("dp")
    fsdp_rank = lax.axis_index("fsdp")
    vocab_rows = embed_table.shape[0]
    local_ids = token_ids - fsdp_rank * vocab_rows
    inside = (local_ids >= 0) & (local_ids < vocab_rows)
    looked = jnp.take(embed_table, jnp.clip(local_ids, 0, vocab_rows - 1), axis=0)
    looked = jnp.where(inside[:, None], looked, jnp.zeros_like(looked))
    inputs = (
        lax.psum_scatter(looked, "fsdp", scatter_dimension=0, tiled=True)
        .astype(jnp.float32)
        .astype(jnp.bfloat16)
    )
    qkv_full, out_full, cent_full = (
        lax.all_gather(w_qkv, "fsdp", axis=0, tiled=True),
        lax.all_gather(w_out, "fsdp", axis=0, tiled=True),
        lax.all_gather(centroids_t, "fsdp", axis=0, tiled=True),
    )
    encoded = encode(inputs, qkv_full, out_full, ln_gain, ln_bias)
    own_rows = encoded.shape[0]
    width = encoded.shape[1]
    block_width = cent_full.shape[1]
    per_dev = block_width // fsdp_size
    slab = lax.all_gather(encoded, "dp", axis=0, tiled=True)
    slab_assign = lax.dynamic_index_in_dim(
        assignments.reshape(dp_size, fsdp_size, own_rows), fsdp_rank, 1, keepdims=False
    ).reshape(-1)
    owned = slab_assign - dp_rank * block_width
    slab_rows = slab.shape[0]
    step_rows = math.gcd(slab_rows, 512)
    columns = jnp.arange(block_width, dtype=jnp.int32)

    def body_visit(totals, pieces):
        block_rows, local = pieces
        logits = jnp.dot(block_rows, cent_full, preferred_element_type=jnp.float32)
        peak = jnp.max(logits, axis=1)
        mass = jnp.sum(jnp.exp(logits - peak[:, None]), axis=1)
        hits = local[:, None] == columns[None, :]
        picked = jnp.sum(jnp.where(hits, logits, 0.0), axis=1)
        return (totals, (peak, mass, picked))

    start = jnp.zeros((1,), jnp.float32)
    partial_value, stats = lax.scan(
        body_visit,
        start,
        (
            slab.reshape(slab_rows // step_rows, step_rows, width),
            owned.reshape(slab_rows // step_rows, step_rows),
        ),
    )
    peaks, masses, picks = (stats[0].reshape(-1), stats[1].reshape(-1), stats[2].reshape(-1))
    peaks, masses, picks = joined((peaks, masses, picks), "dp", combine_parts)
    peak_own = lax.dynamic_slice_in_dim(peaks, dp_rank * own_rows, own_rows)
    mass_own = lax.dynamic_slice_in_dim(masses, dp_rank * own_rows, own_rows)
    pick_own = lax.dynamic_slice_in_dim(picks, dp_rank * own_rows, own_rows)
    token_loss = jnp.log(mass_own) + peak_own - pick_own
    share = lax.all_to_all(encoded, "fsdp", split_axis=1, concat_axis=0, tiled=True)
    every_rows = lax.all_gather(share, "dp", axis=0, tiled=True)
    block_local = assignments - dp_rank * block_width
    partial_share = one_hot_sums(every_rows, block_local, block_width)
    totals = lax.all_to_all(partial_share, "fsdp", split_axis=0, concat_axis=1, tiled=True)
    base = dp_rank * block_width + fsdp_rank * per_dev
    targets = base + jnp.arange(per_dev, dtype=jnp.int32)
    counts = jnp.sum((assignments[:, None] == targets[None, :]).astype(jnp.int32), axis=0)
    previous = lax.dynamic_slice_in_dim(cent_full, fsdp_rank * per_dev, per_dev, 1).T.astype(
        jnp.float32
    )
    new_centroids = jnp.where(
        counts[:, None] > 0, totals / jnp.maximum(counts, 1)[:, None].astype(jnp.float32), previous
    )
    return (token_loss, new_centroids)


VMEM_LIMIT = 60 * 1024 * 1024
WHOLE_VMEM = pl.BlockSpec(memory_space=pltpu.VMEM)


class Place:
    def __init__(self, deep):
        self.deep = deep
        self.dp, self.fsdp = lax.axis_index("dp"), lax.axis_index("fsdp")
        self.x, self.c = self.dp // 2, self.dp % 2
        self.z, self.y = self.fsdp // 2, self.fsdp % 2

    def at(self, x=None, c=None, z=None, y=None):
        x, c = self.x if x is None else x, self.c if c is None else c
        z, y = self.z if z is None else z, self.y if y is None else y
        return {"dp": x * 2 + c, "fsdp": z * 2 + y}

    def greet(self):
        barrier = pltpu.get_barrier_semaphore()
        everyone = 8 * self.deep
        me = self.dp * 2 * self.deep + self.fsdp

        @pl.loop(1, everyone)
        def each(k):
            peer = (me + k) % everyone
            there = {"dp": peer // (2 * self.deep), "fsdp": peer % (2 * self.deep)}
            pl.semaphore_signal(barrier, inc=1, device_id=there, device_id_type=pl.DeviceIdType.MESH)

        pl.semaphore_wait(barrier, everyone - 1)


class Sender:
    def __init__(self, sems):
        self.sems, self.used, self.sent = sems, 0, []

    def send(self, src, dst, recv_sem, peer, when=None):
        copy = pltpu.make_async_remote_copy(
            src_ref=src,
            dst_ref=dst,
            send_sem=self.sems.at[self.used],
            recv_sem=recv_sem,
            device_id=peer,
            device_id_type=pl.DeviceIdType.MESH,
        )
        self.used += 1
        self.sent.append((copy, when))
        guarded(when, copy.start)

    def arrived(self, dst, recv_sem, peer, when=None):
        copy = pltpu.make_async_remote_copy(
            src_ref=dst,
            dst_ref=dst,
            send_sem=self.sems.at[0],
            recv_sem=recv_sem,
            device_id=peer,
            device_id_type=pl.DeviceIdType.MESH,
        )
        guarded(when, copy.wait_recv)

    def drain(self):
        for copy, when in self.sent:
            guarded(when, copy.wait_send)


def guarded(when, action):
    if when is None:
        action()
    else:
        pl.when(when)(action)


def near_first(z, k, deep):
    below, above = z, deep - 1 - z
    both = jnp.minimum(below, above)
    swing = z - (k + 1) // 2 if k % 2 else z + k // 2
    far = jnp.where(above > below, z + k - both, z - k + both)
    return jnp.where(k <= 2 * both, swing, far)


def passage(x, quarters, gain, bias, w_ref):
    width = x.shape[1]

    def dense(rows, q):
        weights = w_ref[q].reshape(width, width)
        return jnp.dot(rows, weights, preferred_element_type=jnp.float32)

    query, key, value = (dense(x, q).astype(jnp.bfloat16) for q in quarters[:3])
    context = []
    for head in range(HEADS):
        at = slice(head * HEAD, (head + 1) * HEAD)
        scores = lax.dot_general(
            query[:, at], key[:, at], (((1,), (1,)), ((), ())), preferred_element_type=jnp.float32
        ) * (1.0 / math.sqrt(HEAD))
        weight = jnp.exp(scores - jnp.max(scores, axis=1, keepdims=True))
        probs = (weight / jnp.sum(weight, axis=1, keepdims=True)).astype(jnp.bfloat16)
        context.append(jnp.dot(probs, value[:, at], preferred_element_type=jnp.float32))
    context = jnp.concatenate(context, axis=1).astype(jnp.bfloat16)
    mixed = dense(context, quarters[3]) + x.astype(jnp.float32)
    return layer_norm(mixed, gain, bias).astype(jnp.bfloat16)


def step_kernel(
    deep,
    ids_ref,
    table_ref,
    qkv_ref,
    out_w_ref,
    norm_ref,
    cent_ref,
    assign_ref,
    loss_ref,
    new_ref,
    rows,
    w,
    from_y,
    joined_y,
    from_z,
    cent,
    old,
    mine,
    tokens,
    counts,
    stat,
    got,
    load_sems,
    send_sems,
    y_sems,
    z_sems,
    w_sems,
    cent_sems,
    token_sems,
    stat_send,
    stat_recv,
):
    place = Place(deep)
    x, c, z, y = place.x, place.c, place.z, place.y
    own = place.fsdp
    parts = 2 * deep
    vocab_rows, width = table_ref.shape
    own_rows = mine.shape[0]
    per_dev = new_ref.shape[0]
    blocks = 4 * parts
    own_block = place.dp * parts + own
    quarter, across = x * 2 + c, (1 - x) * 2 + c
    partner, x_side, y_side = place.at(c=1 - c), place.at(x=1 - x), place.at(y=1 - y)
    up, down = place.at(z=jnp.minimum(z + 1, deep - 1)), place.at(z=jnp.maximum(z - 1, 0))

    loads = []
    for q in range(4):
        part = qkv_ref.at[:, pl.ds(q * width, width)] if q < 3 else out_w_ref
        loads.append(pltpu.make_async_copy(part, w.at[q, own], load_sems.at[q]))
    loads.append(
        pltpu.make_async_copy(
            cent_ref.at[:, pl.ds(pl.multiple_of(own * per_dev, 128), per_dev)], cent.at[own], load_sems.at[4]
        )
    )
    for load in loads:
        load.start()

    def look(y0):
        local = ids_ref[y0] - own * vocab_rows
        hot = local == lax.broadcasted_iota(jnp.int32, (deep * own_rows, vocab_rows), 1)
        found = jnp.dot(
            jnp.where(hot, 1.0, 0.0).astype(jnp.bfloat16), table_ref[...], preferred_element_type=jnp.float32
        )
        rows[y0] = found.astype(jnp.bfloat16).reshape(deep, own_rows, width)

    place.greet()
    out = Sender(send_sems)
    for load in loads:
        load.wait()

    home = w.at[quarter, own]
    out.send(home, home, w_sems.at[quarter, own], up, z + 1 < deep)
    out.send(home, home, w_sems.at[quarter, own], down, z > 0)
    for k in range(1, deep + 1):
        to = (z + k) % deep
        if k == 1:
            look(1 - y)
        out.send(rows.at[1 - y, to], from_y.at[to], y_sems.at[to], y_side)
    look(y)

    def spread(s):
        block = w.at[quarter, s]
        out.send(block, block, w_sems.at[quarter, s], x_side)
        out.send(block, block, w_sems.at[quarter, s], partner)

    def join(k):
        to = (z + k) % deep
        out.arrived(from_y.at[to], y_sems.at[to], y_side)
        joined_y[to] = from_y[to] + rows[y, to]
        if k < deep:
            out.send(joined_y.at[to], from_z.at[deep - k], z_sems.at[deep - k], place.at(z=to))

    for k in range(1, deep):
        z0 = near_first(z, k, deep)
        s = z0 * 2 + y
        block = w.at[quarter, s]
        out.arrived(block, w_sems.at[quarter, s], y_side)
        out.send(block, block, w_sems.at[quarter, s], up, (z0 < z) & (z + 1 < deep))
        out.send(block, block, w_sems.at[quarter, s], down, (z0 > z) & (z > 0))
        spread(s)
    for k in range(1, deep + 1):
        join(k)
    for k in range(deep):
        block = w.at[quarter, near_first(z, k, deep) * 2 + y]
        out.send(block, block, w_sems.at[quarter, near_first(z, k, deep) * 2 + y], y_side)

    def give(z0, y0):
        to = z0 * 2 + y0
        columns = pl.ds(pl.multiple_of(to * per_dev, 128), per_dev)
        out.send(
            cent_ref.at[:, columns], cent.at[own], cent_sems.at[own], {"dp": place.dp, "fsdp": to}
        )

    for k in range(1, deep):
        give((z + k) % deep, y)
    for k in range(deep):
        s = near_first(z, k, deep) * 2 + (1 - y)
        out.arrived(w.at[quarter, s], w_sems.at[quarter, s], y_side)
        spread(s)
    for k in range(deep):
        give((z + k) % deep, 1 - y)
    others = [near_first(z, k, deep) * 2 + y for k in range(1, deep)]
    others += [near_first(z, k, deep) * 2 + (1 - y) for k in range(deep)]
    for s in others:
        block = w.at[across, s]
        out.arrived(block, w_sems.at[across, s], x_side)
        out.send(block, block, w_sems.at[across, s], partner)
    total = joined_y[z]
    for k in range(1, deep):
        out.arrived(from_z.at[k], z_sems.at[k], y_side)
        total = total + from_z[k]
    for q in (x * 2 + (1 - c), (1 - x) * 2 + (1 - c)):
        for s in others:
            out.arrived(w.at[q, s], w_sems.at[q, s], partner)
    for first in range(0, own_rows, SEQ):
        mine[pl.ds(first, SEQ), :] = passage(
            total[first : first + SEQ], range(4), norm_ref[0:1, :], norm_ref[1:2, :], w
        )

    x_first = c == 1
    second_xy = (jnp.where(x_first, 1 - x, x), jnp.where(x_first, y, 1 - y))
    third_xy = (jnp.where(x_first, x, 1 - x), jnp.where(x_first, 1 - y, y))
    second = place.at(x=second_xy[0], y=second_xy[1])
    third = place.at(x=third_xy[0], y=third_xy[1])

    def number(x0, c0, z0, y0):
        return ((x0 * 2 + c0) * deep + z0) * 2 + y0

    def push(b, peer, when=None, src=None):
        block = tokens.at[b]
        out.send(block if src is None else src, block, token_sems.at[b], peer, when)

    def wait(b):
        out.arrived(tokens.at[b], token_sems.at[b], partner)

    push(own_block, up, z + 1 < deep, mine)
    push(own_block, down, z > 0, mine)
    for peer in (second, third, partner):
        push(own_block, peer, None, mine)
    tokens[own_block] = mine[...]
    new_ref[...] = jnp.zeros_like(new_ref)
    counts[...] = jnp.zeros_like(counts)
    base = own_block * per_dev
    centroid = lax.broadcasted_iota(jnp.int32, (per_dev, 2 * own_rows), 0) + base

    def pair_of(p):
        hits = centroid == assign_ref[p]
        return hits, tokens[pl.ds(p * 2, 2)].reshape(2 * own_rows, width)

    def add_up(p):
        hits, some = pair_of(p)
        ones = jnp.where(hits, 1.0, 0.0)
        counts[...] += jnp.sum(ones, axis=1, keepdims=True)
        new_ref[...] += jnp.dot(
            ones.astype(jnp.bfloat16), some, preferred_element_type=jnp.float32
        )

    def score(p):
        hits, some = pair_of(p)
        logits = lax.dot_general(
            old[...], some, (((1,), (1,)), ((), ())), preferred_element_type=jnp.float32
        )
        peak = jnp.max(logits, axis=0, keepdims=True)
        mass = jnp.sum(jnp.exp(logits - peak), axis=0, keepdims=True)
        pick = jnp.sum(jnp.where(hits, logits, 0.0), axis=0, keepdims=True)
        for half in range(2):
            b = p * 2 + half
            at = slice(half * own_rows, (half + 1) * own_rows)
            for k, row in enumerate((peak, mass, pick)):
                stat[b, pl.ds(k, 1), :] = row[:, at]
            pl.when(b != own_block)(stat_copy(b).start)

    def stat_copy(b):
        return pltpu.make_async_remote_copy(
            src_ref=stat.at[b],
            dst_ref=got.at[own_block],
            send_sem=stat_send.at[b],
            recv_sem=stat_recv.at[own_block],
            device_id={"dp": b // parts, "fsdp": b % parts},
            device_id_type=pl.DeviceIdType.MESH,
        )

    def take_centroids():
        for k in range(1, parts):
            s = (own + k) % parts
            out.arrived(cent.at[s], cent_sems.at[s], partner)
        old[...] = cent[...].reshape(width, per_dev).T

    def finish_line(z1):
        for xx, yy in (third_xy, (1 - x, 1 - y)):
            b = number(xx, c, z1, yy)
            wait(b)
            push(b, partner)

    def sums_of(z1, with_scores):
        for x0 in range(2):
            for y0 in range(2):
                wait(number(x0, 1 - c, z1, y0))

        @pl.loop(0, 4)
        def each(i):
            add_up(i * deep + z1)
            if with_scores:
                score(i * deep + z1)

    for k in range(deep):
        z0 = near_first(z, k, deep)
        if k > 0:
            b = number(x, c, z0, y)
            wait(b)
            push(b, up, (z0 < z) & (z + 1 < deep))
            push(b, down, (z0 > z) & (z > 0))
            push(b, second)
            push(b, third)
            push(b, partner)
        b = number(second_xy[0], c, z0, second_xy[1])
        wait(b)
        push(b, third)
        push(b, partner)
        if k >= 1:
            finish_line(near_first(z, k - 1, deep))
        if k == deep - 2:
            take_centroids()
        if k >= 2:
            sums_of(near_first(z, k - 2, deep), True)
    sums_of(near_first(z, deep - 2, deep), True)
    finish_line(near_first(z, deep - 1, deep))
    sums_of(near_first(z, deep - 1, deep), True)

    many = counts[...]
    new_ref[...] = jnp.where(
        many > 0, new_ref[...] / jnp.maximum(many, 1.0), old[...].astype(jnp.float32)
    )
    got[own_block] = stat[own_block]

    @pl.loop(0, blocks)
    def each_device(b):
        @pl.when(b != own_block)
        def done():
            stat_copy(b).wait_send()
            pltpu.make_async_remote_copy(
                src_ref=got.at[b],
                dst_ref=got.at[b],
                send_sem=stat_send.at[b],
                recv_sem=stat_recv.at[b],
                device_id=partner,
                device_id_type=pl.DeviceIdType.MESH,
            ).wait_recv()

    peaks, masses, picks = (got[:, k, :] for k in range(3))
    top = jnp.max(peaks, axis=0, keepdims=True)
    mass = jnp.sum(masses * jnp.exp(peaks - top), axis=0, keepdims=True)
    loss_ref[...] = jnp.log(mass) + top - jnp.sum(picks, axis=0, keepdims=True)
    out.drain()


def token_shards(token_ids, embed_table, w_qkv, w_out, ln_gain, ln_bias, centroids_t, assignments):
    parts = lax.axis_size("fsdp")
    deep = parts // 2
    blocks = 4 * parts
    width = embed_table.shape[1]
    feats = w_qkv.shape[0]
    own_rows = token_ids.shape[0] // parts
    per_dev = centroids_t.shape[1] // parts
    half = jnp.bfloat16
    block = (own_rows, width)
    sems = pltpu.SemaphoreType.DMA
    loss, new = pl.pallas_call(
        functools.partial(step_kernel, deep),
        out_shape=(
            jax.ShapeDtypeStruct((1, own_rows), jnp.float32),
            jax.ShapeDtypeStruct((per_dev, width), jnp.float32),
        ),
        in_specs=[
            WHOLE_VMEM,
            WHOLE_VMEM,
            WHOLE_VMEM,
            WHOLE_VMEM,
            WHOLE_VMEM,
            pl.BlockSpec(memory_space=pl.ANY),
            WHOLE_VMEM,
        ],
        out_specs=(WHOLE_VMEM, WHOLE_VMEM),
        scratch_shapes=[
            pltpu.VMEM((2, deep, *block), half),
            pltpu.VMEM((4, parts, feats, width), half),
            pltpu.VMEM((deep, *block), half),
            pltpu.VMEM((deep, *block), half),
            pltpu.VMEM((deep, *block), half),
            pltpu.VMEM((parts, feats, per_dev), half),
            pltpu.VMEM((per_dev, width), half),
            pltpu.VMEM(block, half),
            pltpu.VMEM((blocks, *block), half),
            pltpu.VMEM((per_dev, 1), jnp.float32),
            pltpu.VMEM((blocks, 8, own_rows), jnp.float32),
            pltpu.VMEM((blocks, 8, own_rows), jnp.float32),
            sems((5,)),
            sems((64 * deep,)),
            sems((deep,)),
            sems((deep,)),
            sems((4, parts)),
            sems((parts,)),
            sems((blocks,)),
            sems((blocks,)),
            sems((blocks,)),
        ],
        compiler_params=pltpu.CompilerParams(
            collective_id=0, has_side_effects=True, vmem_limit_bytes=VMEM_LIMIT
        ),
        name="whole_step",
    )(
        token_ids.reshape(deep, 2, own_rows).transpose(1, 0, 2).reshape(2, deep * own_rows, 1),
        embed_table,
        w_qkv,
        w_out,
        jnp.stack([ln_gain, ln_bias]),
        centroids_t,
        assignments.reshape(blocks // 2, 1, 2 * own_rows),
    )
    return loss.reshape(own_rows), new


def plan(mesh):
    dp_size, fsdp_size = mesh.shape["dp"], mesh.shape["fsdp"]

    def either(*args):
        few_tokens = args[7].shape[0] <= args[6].shape[1]
        paired = dp_size == 4 and fsdp_size % 2 == 0
        return token_shards(*args) if few_tokens and paired else shards(*args)

    return either


def solution(mesh):
    return jax.shard_map(
        plan(mesh),
        mesh=mesh,
        in_specs=(
            P("dp"),
            P("fsdp", None),
            P("fsdp", None),
            P("fsdp", None),
            P(),
            P(),
            P("fsdp", "dp"),
            P(),
        ),
        out_specs=(P(("dp", "fsdp")), P(("dp", "fsdp"), None)),
        check_vma=False,
    )
```
